32 devices in a mesh: doc: 4 (over y, x), cen: 8 (over z, core).
Axes of the slice: x: 2, y: 2, z: 4, core: 2. Of those that a mesh axis runs over, the one named last changes fastest.
Arguments:
- passages: bfloat16 [1536, 1024], P(('doc', 'cen')), may hold values from -64 to 64
- centroids: bfloat16 [8192, 1024], P('cen'), may hold values from -64 to 64
Outputs:
- assign: bfloat16 [1536, 8192], P('doc', 'cen')
- masses: float32 [8192], P('cen')
- new_centroids: float32 [8192, 1024], P('cen', 'doc')
The draws below stay inside these ranges and needn't reach their ends.
All inputs are finite; a program needn't handle non-finite values.
Results may differ from the reference program's by a relative error of at most 0.008.
Values may be sent and summed in bfloat16 or wider, within the bound.
A program may use at most 64 MiB of HBM per device.

```python
import math
import jax
import jax.numpy as jnp
from jax import lax

D = 1024
ITERS = 3
CENTROIDS = 8192
N_ROWS = 1536
N_DOC = 4


def shared_draw(key):
    first_key = jax.random.fold_in(key, 11)
    second_key = jax.random.fold_in(key, 12)
    rows_raw = jax.random.normal(first_key, (N_ROWS, D), jnp.float32)
    cols_raw = jax.random.normal(second_key, (CENTROIDS, D), jnp.float32)
    row_scale = jnp.exp(jax.random.uniform(jax.random.fold_in(key, 13), (N_ROWS, 1), jnp.float32, math.log(0.3), math.log(3.0)))
    col_scale = jnp.exp(jax.random.uniform(jax.random.fold_in(key, 14), (CENTROIDS, 1), jnp.float32, math.log(0.3), math.log(3.0)))
    rows_out = rows_raw * row_scale
    cols_out = cols_raw * col_scale
    return (jnp.clip(rows_out, -64.0, 64.0), jnp.clip(cols_out, -64.0, 64.0))


def draw_passages(key, part):
    return shared_draw(key)[0].astype(jnp.bfloat16)


def draw_centroids(key, part):
    return shared_draw(key)[1].astype(jnp.bfloat16)


def setup_inputs(seed: int = 0) -> dict:
    arg_keys = jax.random.split(jax.random.key(seed), 3)
    return {
        "passages": draw_passages(jax.random.fold_in(arg_keys[2], 71), 0),
        "centroids": draw_centroids(jax.random.fold_in(arg_keys[2], 71), 0),
    }


def reference(passages, centroids):
    scale = 1.0 / math.sqrt(D)
    scores = lax.dot_general(passages, centroids, (((1,), (1,)), ((), ())), preferred_element_type=jnp.float32) * scale
    log_column = math.log(N_ROWS / CENTROIDS)
    col_potential = jnp.zeros((CENTROIDS,), jnp.float32)
    for iteration in range(ITERS):
        row_potential = -jax.nn.logsumexp(scores + col_potential[None, :], axis=1)
        col_potential = log_column - jax.nn.logsumexp(scores + row_potential[:, None], axis=0)
    row_potential = -jax.nn.logsumexp(scores + col_potential[None, :], axis=1)
    weights = jnp.exp(scores + row_potential[:, None] + col_potential[None, :])
    assign = (weights * CENTROIDS).astype(jnp.bfloat16)
    raw_mass = lax.optimization_barrier(jnp.sum(weights, axis=0))
    grouped_assign = assign.reshape(N_DOC, N_ROWS // N_DOC, CENTROIDS)
    grouped_rows = passages.reshape(N_DOC, N_ROWS // N_DOC, D)

    def accumulate(total, pair):
        partial_value = lax.dot_general(pair[0], pair[1], (((0,), (0,)), ((), ())), preferred_element_type=jnp.float32)
        rounded = lax.optimization_barrier(partial_value.astype(jnp.bfloat16))
        return (total + rounded.astype(jnp.float32), 0)
    sums, unused = lax.scan(accumulate, jnp.zeros((CENTROIDS, D), jnp.float32), (grouped_assign, grouped_rows))
    new_centroids = sums / CENTROIDS / raw_mass[:, None]
    masses = raw_mass * CENTROIDS / N_ROWS
    return (assign, masses, new_centroids)
```

```python
import functools
import math

import jax
import jax.numpy as jnp
from jax import lax
from jax.experimental import pallas as pl
from jax.experimental.pallas import tpu as pltpu
from jax.sharding import PartitionSpec as P

ITERS = 3
MESH = pl.DeviceIdType.MESH
LANES = 128


def kernel(
    nd, nc, p_ref, c_ref, assign_out, mass_out, newc_out,
    rows_v, cent_v, scores, rp_v, tbuf, row_slots, col_slots, mass_slots, assign_v, part_send, part_recv, newc_v,
    load_sem, gs_sem, gr_sem, rs_sem, rr_sem, cs_sem, cr_sem, ms_sem, mr_sem, ps_sem, pr_sem, out_sem,
):
    d = lax.axis_index("doc")
    c = lax.axis_index("cen")
    block, width = p_ref.shape
    cols = c_ref.shape[0]
    rows = nc * block
    feats = width // nd
    total_cols = cols * nc
    total_rows = rows * nd
    scale = 1.0 / math.sqrt(width)
    log_column = math.log(total_rows / total_cols)
    sends = []

    load_p = pltpu.make_async_copy(p_ref, rows_v.at[c], load_sem.at[0])
    load_c = pltpu.make_async_copy(c_ref, cent_v, load_sem.at[1])
    load_p.start()
    load_c.start()

    barrier = pltpu.get_barrier_semaphore()
    for k in range(1, nc):
        pl.semaphore_signal(barrier, inc=1, device_id=(d, lax.rem(c + k, nc)), device_id_type=MESH)
    for k in range(1, nd):
        pl.semaphore_signal(barrier, inc=1, device_id=(lax.rem(d + k, nd), c), device_id_type=MESH)
    pl.semaphore_wait(barrier, nc + nd - 2)
    load_p.wait()

    def push(src, dst, send, recv, where):
        copy = pltpu.make_async_remote_copy(
            src_ref=src, dst_ref=dst, send_sem=send, recv_sem=recv, device_id=where, device_id_type=MESH
        )
        copy.start()
        sends.append(copy)

    def arrive(ref, send, recv):
        pltpu.make_async_remote_copy(
            src_ref=ref, dst_ref=ref, send_sem=send, recv_sem=recv, device_id=(d, c), device_id_type=MESH
        ).wait_recv()

    mate = c + 1 - 2 * lax.rem(c, 2)
    half = nc // 2
    for k in range(1, half):
        push(rows_v.at[c], rows_v.at[c], gs_sem.at[k], gr_sem.at[c], (d, lax.rem(c + 2 * k, nc)))
    push(rows_v.at[c], rows_v.at[c], gs_sem.at[0], gr_sem.at[c], (d, mate))
    order = [k for pair in zip(range(1, half), reversed(range(1, half))) for k in pair][: half - 1]
    for k in order:
        src = lax.rem(c + nc - 2 * k, nc)
        arrive(rows_v.at[src], gs_sem.at[half + k], gr_sem.at[src])
        push(rows_v.at[src], rows_v.at[src], gs_sem.at[half + k], gr_sem.at[src], (d, mate))
    arrive(rows_v.at[mate], gs_sem.at[0], gr_sem.at[mate])
    for k in range(1, half):
        src = lax.rem(mate + nc - 2 * k, nc)
        arrive(rows_v.at[src], gs_sem.at[0], gr_sem.at[src])
    load_c.wait()

    group_rows = rows_v[...].reshape(rows, width)
    tile = min(256, cols)
    for j in range(cols // tile):
        at = slice(j * tile, (j + 1) * tile)
        scores[:, at] = (
            lax.dot_general(
                group_rows, cent_v[at, :], (((1,), (1,)), ((), ())), preferred_element_type=jnp.float32
            )
            * scale
        )

    step_rows = 64
    lane = lax.broadcasted_iota(jnp.int32, (step_rows, LANES), 1)

    def combine(slots, r, n):
        peak = slots[r, 0, 0:1, :]
        for k in range(1, n):
            peak = jnp.maximum(peak, slots[r, k, 0:1, :])
        total = jnp.zeros_like(peak)
        for k in range(n):
            total = total + slots[r, k, 1:2, :] * jnp.exp(slots[r, k, 0:1, :] - peak)
        return peak + jnp.log(total)

    def row_round(r, col_potential):
        @pl.loop(0, rows // step_rows)
        def _(i):
            at = pl.ds(pl.multiple_of(i * step_rows, step_rows), step_rows)
            x = scores[at, :]
            if col_potential is not None:
                x = x + col_potential
            m = jnp.max(x, axis=1, keepdims=True)
            s = jnp.sum(jnp.exp(x - m), axis=1, keepdims=True)
            tbuf[at, :] = jnp.where(lane == 0, m, s)

        row_slots[r, c, :, :] = tbuf[...].T[0:2, :]
        for k in range(1, nc):
            push(row_slots.at[r, c], row_slots.at[r, c], rs_sem.at[r, k], rr_sem.at[r, c], (d, lax.rem(c + k, nc)))
        for k in range(1, nc):
            src = lax.rem(c + nc - k, nc)
            arrive(row_slots.at[r, src], rs_sem.at[r, k], rr_sem.at[r, src])
        row_potential = -combine(row_slots, r, nc)
        rp_v[...] = jnp.broadcast_to(row_potential, (LANES, rows)).T

    def col_round(r):
        for j in range(cols // LANES):
            at = slice(j * LANES, (j + 1) * LANES)
            x = scores[:, at] + rp_v[...]
            m = jnp.max(x, axis=0, keepdims=True)
            s = jnp.sum(jnp.exp(x - m), axis=0, keepdims=True)
            col_slots[r, d, 0:1, at] = m
            col_slots[r, d, 1:2, at] = s
        for k in range(1, nd):
            push(col_slots.at[r, d], col_slots.at[r, d], cs_sem.at[r, k], cr_sem.at[r, d], (lax.rem(d + k, nd), c))
        for k in range(1, nd):
            src = lax.rem(d + nd - k, nd)
            arrive(col_slots.at[r, src], cs_sem.at[r, k], cr_sem.at[r, src])
        return log_column - combine(col_slots, r, nd)

    col_potential = None
    for r in range(ITERS):
        row_round(r, col_potential)
        col_potential = col_round(r)
    row_round(ITERS, col_potential)

    for j in range(cols // LANES):
        at = slice(j * LANES, (j + 1) * LANES)
        w = jnp.exp(scores[:, at] + rp_v[...] + col_potential[:, at])
        mass_slots[d, :, at] = jnp.sum(w, axis=0, keepdims=True)
        assign_v[:, at] = (w * total_cols).astype(jnp.bfloat16)
    assign_copy = pltpu.make_async_copy(assign_v, assign_out, out_sem.at[0])
    assign_copy.start()
    for k in range(1, nd):
        push(mass_slots.at[d], mass_slots.at[d], ms_sem.at[k], mr_sem.at[d], (lax.rem(d + k, nd), c))

    def partial(q):
        r3 = rows_v[:, :, pl.ds(pl.multiple_of(q * feats, feats), feats)].reshape(rows, feats)
        return lax.dot_general(
            assign_v[...], r3, (((0,), (0,)), ((), ())), preferred_element_type=jnp.float32
        ).astype(jnp.bfloat16)

    for k in reversed(range(1, nd)):
        q = lax.rem(d + k, nd)
        part_send[k, :, :] = partial(q)
        push(part_send.at[k], part_recv.at[d], ps_sem.at[k], pr_sem.at[d], (q, c))
    part_recv[d, :, :] = partial(d)

    for k in range(1, nd):
        src = lax.rem(d + nd - k, nd)
        arrive(mass_slots.at[src], ms_sem.at[k], mr_sem.at[src])
    raw_mass = mass_slots[0]
    for k in range(1, nd):
        raw_mass = raw_mass + mass_slots[k]
    mass_out[...] = raw_mass * total_cols / total_rows
    mass_col = jnp.broadcast_to(raw_mass, (LANES, cols)).T

    for k in range(1, nd):
        src = lax.rem(d + nd - k, nd)
        arrive(part_recv.at[src], ps_sem.at[k], pr_sem.at[src])
    for j in range(feats // LANES):
        at = slice(j * LANES, (j + 1) * LANES)
        sums = part_recv[0, :, at].astype(jnp.float32)
        for k in range(1, nd):
            sums = sums + part_recv[k, :, at].astype(jnp.float32)
        newc_v[:, at] = sums / total_cols / mass_col
    newc_copy = pltpu.make_async_copy(newc_v, newc_out, out_sem.at[1])
    newc_copy.start()
    for copy in sends:
        copy.wait_send()
    assign_copy.wait()
    newc_copy.wait()


SPLIT_ROUNDS = 1


def wide_kernel(
    nd, nc, p_ref, c_ref, e_out, own_out, pt_out, f_out,
    rows_v, cent_v, scores, rexp, row_slots, col_slots, cm, cs,
    load_sem, gs_sem, gr_sem, ds_sem, dr_sem, rs_sem, rr_sem, cs_sem, cr_sem,
):
    d = lax.axis_index("doc")
    c = lax.axis_index("cen")
    block, width = p_ref.shape
    cols = c_ref.shape[0]
    rows = nc * block
    feats = width // nd
    scale = math.log2(math.e) / math.sqrt(width)
    log_column = math.log2(rows * nd / (cols * nc))
    sends = []
    mate = c + 1 - 2 * lax.rem(c, 2)
    half = nc // 2
    beside = d + 1 - 2 * lax.rem(d, 2)
    docs = [d, beside, lax.rem(d + 2, nd), lax.rem(beside + 2, nd)]

    barrier = pltpu.get_barrier_semaphore()
    for k in range(1, nc):
        pl.semaphore_signal(barrier, inc=1, device_id=(d, lax.rem(c + k, nc)), device_id_type=MESH)
    for q in range(1, nd):
        pl.semaphore_signal(barrier, inc=1, device_id=(docs[q], c), device_id_type=MESH)
    load_p = pltpu.make_async_copy(p_ref, rows_v.at[0, c], load_sem.at[0])
    load_c = pltpu.make_async_copy(c_ref, cent_v, load_sem.at[1])
    load_p.start()
    load_c.start()
    pl.semaphore_wait(barrier, nc + nd - 2)

    def push(src, dst, send, recv, where):
        copy = pltpu.make_async_remote_copy(
            src_ref=src, dst_ref=dst, send_sem=send, recv_sem=recv, device_id=where, device_id_type=MESH
        )
        copy.start()
        sends.append(copy)

    def arrive(ref, send, recv):
        pltpu.make_async_remote_copy(
            src_ref=ref, dst_ref=ref, send_sem=send, recv_sem=recv, device_id=(d, c), device_id_type=MESH
        ).wait_recv()

    def to_docs(src, b, slot):
        for q in range(1, nd):
            push(src, rows_v.at[q, b], ds_sem.at[q, slot], dr_sem.at[q, b], (docs[q], c))

    for k in range(1, half):
        push(p_ref, rows_v.at[0, c], gs_sem.at[k], gr_sem.at[c], (d, lax.rem(c + 2 * k, nc)))
    push(p_ref, rows_v.at[0, c], gs_sem.at[0], gr_sem.at[c], (d, mate))
    to_docs(p_ref, c, 0)
    order = [k for pair in zip(range(1, half), reversed(range(1, half))) for k in pair][: half - 1]
    for k in order:
        src = lax.rem(c + nc - 2 * k, nc)
        got = rows_v.at[0, src]
        arrive(got, gs_sem.at[half + k], gr_sem.at[src])
        push(got, got, gs_sem.at[half + k], gr_sem.at[src], (d, mate))
        to_docs(got, src, k)
    load_p.wait()
    load_c.wait()
    arrive(rows_v.at[0, mate], gs_sem.at[0], gr_sem.at[mate])
    for k in range(1, half):
        src = lax.rem(mate + nc - 2 * k, nc)
        arrive(rows_v.at[0, src], gs_sem.at[0], gr_sem.at[src])

    def relay(k):
        b = lax.rem(c + nc - 2 * k, nc)
        for q in range(1, nd):
            got = rows_v.at[q, b]
            arrive(got, ds_sem.at[0, k], dr_sem.at[q, b])
            push(got, got, ds_sem.at[nd + q, k], dr_sem.at[q, b], (d, mate))

    def arrive_doc(q):
        for k in range(half):
            b = lax.rem(mate + nc - 2 * k, nc)
            arrive(rows_v.at[q, b], ds_sem.at[0, k], dr_sem.at[q, b])

    tile = min(256, cols)

    def score(q):
        for j in range(cols // tile):
            at = slice(j * tile, (j + 1) * tile)
            scores[q, :, at] = (
                lax.dot_general(
                    rows_v[q].reshape(rows, width),
                    cent_v[at, :],
                    (((1,), (1,)), ((), ())),
                    preferred_element_type=jnp.float32,
                )
                * scale
            )

    def widen(x):
        return jnp.broadcast_to(x, (LANES, x.shape[1])).T

    step_rows = 32

    def row_stats(q, r, col_potential):
        for g in range(rows // LANES):
            parts = []
            for i in range(g * LANES, (g + 1) * LANES, step_rows):
                xs = []
                for j in range(0, cols, LANES):
                    x = scores[q, i : i + step_rows, j : j + LANES]
                    if col_potential is not None:
                        x = x + col_potential[:, j : j + LANES]
                    xs.append(x)
                m = functools.reduce(jnp.maximum, xs)
                s = functools.reduce(jnp.add, [jnp.exp2(x - m) for x in xs])
                parts.append(m + jnp.log2(s))
            t = jnp.concatenate(parts, axis=0).T
            m = jnp.max(t, axis=0, keepdims=True)
            s = jnp.sum(jnp.exp2(t - m), axis=0, keepdims=True)
            row_slots[r, q, c, :, g * LANES : (g + 1) * LANES] = m + jnp.log2(s)
        mine = row_slots.at[r, q, c]
        for k in range(1, nc):
            push(mine, mine, rs_sem.at[r, q, k], rr_sem.at[r, q, c], (d, lax.rem(c + k, nc)))

    def join(parts):
        peak = functools.reduce(jnp.maximum, parts)
        return peak + jnp.log2(functools.reduce(jnp.add, [jnp.exp2(x - peak) for x in parts]))

    def row_potential(q, r):
        for k in range(1, nc):
            src = lax.rem(c + nc - k, nc)
            arrive(row_slots.at[r, q, src], rs_sem.at[r, q, 0], rr_sem.at[r, q, src])
        return -join([row_slots[r, q, k] for k in range(nc)])

    def col_part(q, r):
        rexp[...] = widen(row_potential(q, r))
        for j in range(0, cols, LANES):
            ms, ss = [], []
            for i in range(0, rows, LANES):
                x = scores[q, i : i + LANES, j : j + LANES] + rexp[i : i + LANES, :]
                x = x.reshape(LANES // 8, 8, LANES)
                m = jnp.max(x, axis=0)
                ms.append(m)
                ss.append(jnp.sum(jnp.exp2(x - m[None]), axis=0))
            m = functools.reduce(jnp.maximum, ms)
            cm[q, :, j : j + LANES] = m
            cs[q, :, j : j + LANES] = functools.reduce(jnp.add, [s * jnp.exp2(a - m) for a, s in zip(ms, ss)])

    def col_merge(n):
        peak = jnp.max(jnp.max(cm[0:n], axis=0), axis=0, keepdims=True)
        total = functools.reduce(jnp.add, [cs[q] * jnp.exp2(cm[q] - peak) for q in range(n)])
        return peak + jnp.log2(jnp.sum(total, axis=0, keepdims=True))

    def split_round(r, col_potential, before, after):
        row_stats(0, r, col_potential)
        before()
        col_part(0, r)
        col_slots[r, 0] = col_merge(1)
        for q in range(1, nd):
            push(col_slots.at[r, 0], col_slots.at[r, q], cs_sem.at[r, q], cr_sem.at[r, q], (docs[q], c))
        after()
        for q in range(1, nd):
            arrive(col_slots.at[r, q], cs_sem.at[r, 0], cr_sem.at[r, q])
        return log_column - join([col_slots[r, q] for q in range(nd)])

    def whole_round(r, col_potential):
        for q in range(nd):
            if r == SPLIT_ROUNDS and q:
                arrive_doc(q)
                score(q)
            row_stats(q, r, col_potential)
        for q in range(nd):
            col_part(q, r)
        return log_column - col_merge(nd)

    score(0)
    col_potential = None
    for r in range(SPLIT_ROUNDS):
        col_potential = split_round(
            r, col_potential, lambda: relay(0), lambda: [relay(k) for k in order] and None
        )
    for r in range(SPLIT_ROUNDS, ITERS):
        col_potential = whole_round(r, col_potential)

    for q in range(nd):
        row_stats(q, ITERS, col_potential)
    my_feats = pl.ds(pl.multiple_of(d * feats, feats), feats)
    for q in range(nd):
        rexp[...] = widen(row_slots[ITERS, q, c])
        for j in range(0, cols, LANES):
            at = slice(j, j + LANES)
            e = jnp.exp2(scores[q, :, at] + col_potential[:, at] - rexp[...])
            e_out[q, :, at] = e.astype(jnp.bfloat16)
            if not q:
                own_out[:, at] = e
        pt_out[q] = rows_v[q, :, :, my_feats].reshape(rows, feats).T
    for q in range(nd):
        f_out[q] = jnp.exp2(row_slots[ITERS, q, c] + row_potential(q, ITERS))
    for copy in sends:
        copy.wait_send()


def finish_kernel(
    total_rows, total_cols, e_ref, own_ref, pt_ref, f_ref, assign_out, mass_out, newc_out,
    assign_v, lhs, acc, mass_v, newc_v, out_sem,
):
    nd, rows, cols = e_ref.shape
    feats = pt_ref.shape[1]
    f_own = jnp.broadcast_to(f_ref[0] * total_cols, (LANES, rows)).T
    for j in range(0, cols, LANES):
        at = slice(j, j + LANES)
        assign_v[:, at] = (own_ref[:, at] * f_own).astype(jnp.bfloat16)
    assign_copy = pltpu.make_async_copy(assign_v, assign_out, out_sem.at[0])
    assign_copy.start()
    pad = lhs.shape[1] - feats
    lane = lax.broadcasted_iota(jnp.int32, (pad, rows), 0)
    for q in range(nd):
        f = f_ref[q]
        lhs[q, 0:feats, :] = (pt_ref[q].astype(jnp.float32) * f).astype(jnp.bfloat16)
        high = f.astype(jnp.bfloat16).astype(jnp.float32)
        lhs[q, feats:, :] = jnp.where(lane == 0, high, jnp.where(lane == 1, f - high, 0.0)).astype(jnp.bfloat16)
    tile = min(256, cols)
    for j in range(0, cols, tile):
        at = slice(j, j + tile)
        total = None
        for q in range(nd):
            part = lax.dot_general(
                lhs[q], e_ref[q, :, at], (((1,), (0,)), ((), ())), preferred_element_type=jnp.float32
            )
            total = part if total is None else total + part
        acc[:, at] = total
    copies = []
    for j in range(0, cols, LANES):
        at = slice(j, j + LANES)
        mass = acc[feats : feats + 1, at] + acc[feats + 1 : feats + 2, at]
        mass_v[j // LANES : j // LANES + 1, :] = mass * total_cols / total_rows
        newc_v[at, :] = (acc[0:feats, at] / mass).T
        if (j + LANES) % (2 * LANES) == 0:
            part = pl.ds(j - LANES, 2 * LANES)
            copy = pltpu.make_async_copy(newc_v.at[part], newc_out.at[part], out_sem.at[2 + j // (2 * LANES)])
            copy.start()
            copies.append(copy)
    mass_copy = pltpu.make_async_copy(mass_v, mass_out, out_sem.at[1])
    mass_copy.start()
    assign_copy.wait()
    for copy in copies:
        copy.wait()
    mass_copy.wait()


def wide_shards(nd, nc, passages, centroids):
    block, width = passages.shape
    cols = centroids.shape[0]
    rows = nc * block
    feats = width // nd
    dma = pltpu.SemaphoreType.DMA
    f32, bf16 = jnp.float32, jnp.bfloat16
    vmem = pl.BlockSpec(memory_space=pltpu.VMEM)
    any_spec = pl.BlockSpec(memory_space=pl.ANY)
    e, own, pt, f = pl.pallas_call(
        functools.partial(wide_kernel, nd, nc),
        out_shape=(
            jax.ShapeDtypeStruct((nd, rows, cols), bf16),
            jax.ShapeDtypeStruct((rows, cols), f32),
            jax.ShapeDtypeStruct((nd, feats, rows), bf16),
            jax.ShapeDtypeStruct((nd, 1, rows), f32),
        ),
        in_specs=[pl.BlockSpec(memory_space=pltpu.MemorySpace.HBM)] * 2,
        out_specs=(vmem,) * 4,
        scratch_shapes=[
            pltpu.VMEM((nd, nc, block, width), bf16),
            pltpu.VMEM((cols, width), bf16),
            pltpu.VMEM((nd, rows, cols), f32),
            pltpu.VMEM((rows, LANES), f32),
            pltpu.VMEM((ITERS + 1, nd, nc, 1, rows), f32),
            pltpu.VMEM((ITERS, nd, 1, cols), f32),
            pltpu.VMEM((nd, 8, cols), f32),
            pltpu.VMEM((nd, 8, cols), f32),
            dma((2,)),
            dma((nc,)),
            dma((nc,)),
            dma((2 * nd, nc // 2)),
            dma((nd, nc)),
            dma((ITERS + 1, nd, nc)),
            dma((ITERS + 1, nd, nc)),
            dma((ITERS, nd)),
            dma((ITERS, nd)),
        ],
        compiler_params=pltpu.CompilerParams(
            collective_id=0, has_side_effects=True, vmem_limit_bytes=44 * 1024 * 1024
        ),
    )(passages, centroids)
    pad = 16
    assign, masses, newc = pl.pallas_call(
        functools.partial(finish_kernel, rows * nd, cols * nc),
        out_shape=(
            jax.ShapeDtypeStruct((rows, cols), bf16),
            jax.ShapeDtypeStruct((cols // LANES, LANES), f32),
            jax.ShapeDtypeStruct((cols, feats), f32),
        ),
        in_specs=[vmem] * 4,
        out_specs=(any_spec,) * 3,
        scratch_shapes=[
            pltpu.VMEM((rows, cols), bf16),
            pltpu.VMEM((nd, feats + pad, rows), bf16),
            pltpu.VMEM((feats + pad, cols), f32),
            pltpu.VMEM((cols // LANES, LANES), f32),
            pltpu.VMEM((cols, feats), f32),
            dma((2 + cols // (2 * LANES),)),
        ],
        compiler_params=pltpu.CompilerParams(vmem_limit_bytes=32 * 1024 * 1024),
    )(e, own, pt, f)
    return assign, masses.reshape(cols), newc


def shards(nd, nc, passages, centroids):
    block, width = passages.shape
    cols = centroids.shape[0]
    rows = nc * block
    feats = width // nd
    if nd == 4 and nc % 2 == 0 and nc > 2 and nd * rows * cols <= 2**21 and rows % LANES == 0 and cols % 256 == 0:
        return wide_shards(nd, nc, passages, centroids)
    any_spec = pl.BlockSpec(memory_space=pl.ANY)
    dma = pltpu.SemaphoreType.DMA
    f32, bf16 = jnp.float32, jnp.bfloat16
    assign, masses, newc = pl.pallas_call(
        functools.partial(kernel, nd, nc),
        out_shape=(
            jax.ShapeDtypeStruct((rows, cols), bf16),
            jax.ShapeDtypeStruct((1, cols), f32),
            jax.ShapeDtypeStruct((cols, feats), f32),
        ),
        in_specs=[pl.BlockSpec(memory_space=pltpu.MemorySpace.HBM)] * 2,
        out_specs=(any_spec, pl.BlockSpec(memory_space=pltpu.VMEM), any_spec),
        scratch_shapes=[
            pltpu.VMEM((nc, block, width), bf16),
            pltpu.VMEM((cols, width), bf16),
            pltpu.VMEM((rows, cols), f32),
            pltpu.VMEM((rows, LANES), f32),
            pltpu.VMEM((rows, LANES), f32),
            pltpu.VMEM((ITERS + 1, nc, 2, rows), f32),
            pltpu.VMEM((ITERS, nd, 2, cols), f32),
            pltpu.VMEM((nd, 1, cols), f32),
            pltpu.VMEM((rows, cols), bf16),
            pltpu.VMEM((nd, cols, feats), bf16),
            pltpu.VMEM((nd, cols, feats), bf16),
            pltpu.VMEM((cols, feats), f32),
            dma((2,)),
            dma((nc,)),
            dma((nc,)),
            dma((ITERS + 1, nc)),
            dma((ITERS + 1, nc)),
            dma((ITERS, nd)),
            dma((ITERS, nd)),
            dma((nd,)),
            dma((nd,)),
            dma((nd,)),
            dma((nd,)),
            dma((2,)),
        ],
        compiler_params=pltpu.CompilerParams(
            collective_id=0, has_side_effects=True, vmem_limit_bytes=52 * 1024 * 1024
        ),
    )(passages, centroids)
    return assign, masses.reshape(cols), newc


def solution(mesh):
    nd, nc = mesh.shape["doc"], mesh.shape["cen"]
    in_specs = (P(("doc", "cen"), None), P("cen", None))
    out_specs = (P("doc", "cen"), P("cen"), P("cen", "doc"))
    return jax.shard_map(
        functools.partial(shards, nd, nc), mesh=mesh, in_specs=in_specs, out_specs=out_specs, check_vma=False
    )
```

```python
import functools
import math

import jax
import jax.numpy as jnp
from jax import lax
from jax.experimental import pallas as pl
from jax.experimental.pallas import tpu as pltpu
from jax.sharding import PartitionSpec as P

ITERS = 3
MESH = pl.DeviceIdType.MESH
LANES = 128


def kernel(
    nd, nc, p_ref, c_ref, assign_out, mass_out, newc_out,
    rows_v, cent_v, scores, rp_v, tbuf, row_slots, col_slots, mass_slots, assign_v, part_send, part_recv, newc_v,
    load_sem, gs_sem, gr_sem, rs_sem, rr_sem, cs_sem, cr_sem, ms_sem, mr_sem, ps_sem, pr_sem, out_sem,
):
    d = lax.axis_index("doc")
    c = lax.axis_index("cen")
    block, width = p_ref.shape
    cols = c_ref.shape[0]
    rows = nc * block
    feats = width // nd
    total_cols = cols * nc
    total_rows = rows * nd
    scale = 1.0 / math.sqrt(width)
    log_column = math.log(total_rows / total_cols)
    sends = []

    load_p = pltpu.make_async_copy(p_ref, rows_v.at[c], load_sem.at[0])
    load_c = pltpu.make_async_copy(c_ref, cent_v, load_sem.at[1])
    load_p.start()
    load_c.start()

    barrier = pltpu.get_barrier_semaphore()
    for k in range(1, nc):
        pl.semaphore_signal(barrier, inc=1, device_id=(d, lax.rem(c + k, nc)), device_id_type=MESH)
    for k in range(1, nd):
        pl.semaphore_signal(barrier, inc=1, device_id=(lax.rem(d + k, nd), c), device_id_type=MESH)
    pl.semaphore_wait(barrier, nc + nd - 2)
    load_p.wait()

    def push(src, dst, send, recv, where):
        copy = pltpu.make_async_remote_copy(
            src_ref=src, dst_ref=dst, send_sem=send, recv_sem=recv, device_id=where, device_id_type=MESH
        )
        copy.start()
        sends.append(copy)

    def arrive(ref, send, recv):
        pltpu.make_async_remote_copy(
            src_ref=ref, dst_ref=ref, send_sem=send, recv_sem=recv, device_id=(d, c), device_id_type=MESH
        ).wait_recv()

    mate = c + 1 - 2 * lax.rem(c, 2)
    half = nc // 2
    for k in range(1, half):
        push(rows_v.at[c], rows_v.at[c], gs_sem.at[k], gr_sem.at[c], (d, lax.rem(c + 2 * k, nc)))
    push(rows_v.at[c], rows_v.at[c], gs_sem.at[0], gr_sem.at[c], (d, mate))
    order = [k for pair in zip(range(1, half), reversed(range(1, half))) for k in pair][: half - 1]
    for k in order:
        src = lax.rem(c + nc - 2 * k, nc)
        arrive(rows_v.at[src], gs_sem.at[half + k], gr_sem.at[src])
        push(rows_v.at[src], rows_v.at[src], gs_sem.at[half + k], gr_sem.at[src], (d, mate))
    arrive(rows_v.at[mate], gs_sem.at[0], gr_sem.at[mate])
    for k in range(1, half):
        src = lax.rem(mate + nc - 2 * k, nc)
        arrive(rows_v.at[src], gs_sem.at[0], gr_sem.at[src])
    load_c.wait()

    group_rows = rows_v[...].reshape(rows, width)
    tile = min(256, cols)
    for j in range(cols // tile):
        at = slice(j * tile, (j + 1) * tile)
        scores[:, at] = (
            lax.dot_general(
                group_rows, cent_v[at, :], (((1,), (1,)), ((), ())), preferred_element_type=jnp.float32
            )
            * scale
        )

    step_rows = 64
    lane = lax.broadcasted_iota(jnp.int32, (step_rows, LANES), 1)

    def combine(slots, r, n):
        peak = slots[r, 0, 0:1, :]
        for k in range(1, n):
            peak = jnp.maximum(peak, slots[r, k, 0:1, :])
        total = jnp.zeros_like(peak)
        for k in range(n):
            total = total + slots[r, k, 1:2, :] * jnp.exp(slots[r, k, 0:1, :] - peak)
        return peak + jnp.log(total)

    def row_round(r, col_potential):
        @pl.loop(0, rows // step_rows)
        def _(i):
            at = pl.ds(pl.multiple_of(i * step_rows, step_rows), step_rows)
            x = scores[at, :]
            if col_potential is not None:
                x = x + col_potential
            m = jnp.max(x, axis=1, keepdims=True)
            s = jnp.sum(jnp.exp(x - m), axis=1, keepdims=True)
            tbuf[at, :] = jnp.where(lane == 0, m, s)

        row_slots[r, c, :, :] = tbuf[...].T[0:2, :]
        for k in range(1, nc):
            push(row_slots.at[r, c], row_slots.at[r, c], rs_sem.at[r, k], rr_sem.at[r, c], (d, lax.rem(c + k, nc)))
        for k in range(1, nc):
            src = lax.rem(c + nc - k, nc)
            arrive(row_slots.at[r, src], rs_sem.at[r, k], rr_sem.at[r, src])
        row_potential = -combine(row_slots, r, nc)
        rp_v[...] = jnp.broadcast_to(row_potential, (LANES, rows)).T

    def col_round(r):
        for j in range(cols // LANES):
            at = slice(j * LANES, (j + 1) * LANES)
            x = scores[:, at] + rp_v[...]
            m = jnp.max(x, axis=0, keepdims=True)
            s = jnp.sum(jnp.exp(x - m), axis=0, keepdims=True)
            col_slots[r, d, 0:1, at] = m
            col_slots[r, d, 1:2, at] = s
        for k in range(1, nd):
            push(col_slots.at[r, d], col_slots.at[r, d], cs_sem.at[r, k], cr_sem.at[r, d], (lax.rem(d + k, nd), c))
        for k in range(1, nd):
            src = lax.rem(d + nd - k, nd)
            arrive(col_slots.at[r, src], cs_sem.at[r, k], cr_sem.at[r, src])
        return log_column - combine(col_slots, r, nd)

    col_potential = None
    for r in range(ITERS):
        row_round(r, col_potential)
        col_potential = col_round(r)
    row_round(ITERS, col_potential)

    for j in range(cols // LANES):
        at = slice(j * LANES, (j + 1) * LANES)
        w = jnp.exp(scores[:, at] + rp_v[...] + col_potential[:, at])
        mass_slots[d, :, at] = jnp.sum(w, axis=0, keepdims=True)
        assign_v[:, at] = (w * total_cols).astype(jnp.bfloat16)
    assign_copy = pltpu.make_async_copy(assign_v, assign_out, out_sem.at[0])
    assign_copy.start()
    for k in range(1, nd):
        push(mass_slots.at[d], mass_slots.at[d], ms_sem.at[k], mr_sem.at[d], (lax.rem(d + k, nd), c))

    def partial(q):
        r3 = rows_v[:, :, pl.ds(pl.multiple_of(q * feats, feats), feats)].reshape(rows, feats)
        return lax.dot_general(
            assign_v[...], r3, (((0,), (0,)), ((), ())), preferred_element_type=jnp.float32
        ).astype(jnp.bfloat16)

    for k in reversed(range(1, nd)):
        q = lax.rem(d + k, nd)
        part_send[k, :, :] = partial(q)
        push(part_send.at[k], part_recv.at[d], ps_sem.at[k], pr_sem.at[d], (q, c))
    part_recv[d, :, :] = partial(d)

    for k in range(1, nd):
        src = lax.rem(d + nd - k, nd)
        arrive(mass_slots.at[src], ms_sem.at[k], mr_sem.at[src])
    raw_mass = mass_slots[0]
    for k in range(1, nd):
        raw_mass = raw_mass + mass_slots[k]
    mass_out[...] = raw_mass * total_cols / total_rows
    mass_col = jnp.broadcast_to(raw_mass, (LANES, cols)).T

    for k in range(1, nd):
        src = lax.rem(d + nd - k, nd)
        arrive(part_recv.at[src], ps_sem.at[k], pr_sem.at[src])
    for j in range(feats // LANES):
        at = slice(j * LANES, (j + 1) * LANES)
        sums = part_recv[0, :, at].astype(jnp.float32)
        for k in range(1, nd):
            sums = sums + part_recv[k, :, at].astype(jnp.float32)
        newc_v[:, at] = sums / total_cols / mass_col
    newc_copy = pltpu.make_async_copy(newc_v, newc_out, out_sem.at[1])
    newc_copy.start()
    for copy in sends:
        copy.wait_send()
    assign_copy.wait()
    newc_copy.wait()


SPLIT_ROUNDS = 2


def wide_kernel(
    nd, nc, p_ref, c_ref, assign_out, acc_out,
    rows_v, cent_v, cent_t, e_v, own_v, pt_v, lhs, scores, rexp, row_slots, col_slots, cm, cs,
    load_sem, gs_sem, gr_sem, ds_sem, dr_sem, rs_sem, rr_sem, cs_sem, cr_sem,
):
    d = lax.axis_index("doc")
    c = lax.axis_index("cen")
    block, width = p_ref.shape
    cols = c_ref.shape[0]
    rows = nc * block
    feats = width // nd
    scale = math.log2(math.e) / math.sqrt(width)
    log_column = math.log2(rows * nd / (cols * nc))
    sends = []
    mate = c + 1 - 2 * lax.rem(c, 2)
    half = nc // 2
    beside = d + 1 - 2 * lax.rem(d, 2)
    docs = [d, beside, lax.rem(d + 2, nd), lax.rem(beside + 2, nd)]

    barrier = pltpu.get_barrier_semaphore()
    for k in range(1, nc):
        pl.semaphore_signal(barrier, inc=1, device_id=(d, lax.rem(c + k, nc)), device_id_type=MESH)
    for q in range(1, nd):
        pl.semaphore_signal(barrier, inc=1, device_id=(docs[q], c), device_id_type=MESH)
    load_p = pltpu.make_async_copy(p_ref, rows_v.at[0, c], load_sem.at[0])
    load_c = pltpu.make_async_copy(c_ref, cent_v, load_sem.at[1])
    load_p.start()
    load_c.start()
    pl.semaphore_wait(barrier, nc + nd - 2)

    def push(src, dst, send, recv, where):
        copy = pltpu.make_async_remote_copy(
            src_ref=src, dst_ref=dst, send_sem=send, recv_sem=recv, device_id=where, device_id_type=MESH
        )
        copy.start()
        sends.append(copy)

    def arrive(ref, send, recv):
        pltpu.make_async_remote_copy(
            src_ref=ref, dst_ref=ref, send_sem=send, recv_sem=recv, device_id=(d, c), device_id_type=MESH
        ).wait_recv()

    z = c // 2
    near = c + 2 - 4 * lax.rem(z, 2)
    blocks = [c, near, lax.rem(c + half, nc), lax.rem(near + half, nc)]
    mates = [b + mate - c for b in blocks]
    tile = min(256, cols)

    def to_docs(src, k):
        for q in range(1, nd):
            push(src, rows_v.at[q, blocks[k]], ds_sem.at[q, k], dr_sem.at[q, blocks[k]], (docs[q], c))

    def take_block(k):
        got = rows_v.at[0, blocks[k]]
        arrive(got, gs_sem.at[half + k], gr_sem.at[blocks[k]])
        push(got, got, gs_sem.at[half + k], gr_sem.at[blocks[k]], (d, mate))
        to_docs(got, k)

    def take_mate(k):
        arrive(rows_v.at[0, mates[k]], gs_sem.at[0], gr_sem.at[mates[k]])

    def score_half(h):
        x = rows_v[0, pl.ds(h * half, half)].reshape(rows // 2, width)
        to = pl.ds(pl.multiple_of(h * (rows // 2), 32), rows // 2)
        for j in range(0, cols, tile):
            at = slice(j, j + tile)
            scores[0, to, at] = jnp.dot(x, cent_t[:, at], preferred_element_type=jnp.float32) * scale

    for k in range(1, half):
        push(p_ref, rows_v.at[0, c], gs_sem.at[k], gr_sem.at[c], (d, blocks[k]))
    push(p_ref, rows_v.at[0, c], gs_sem.at[0], gr_sem.at[c], (d, mate))
    to_docs(p_ref, 0)
    load_c.wait()
    cent_t[...] = cent_v[...].T
    load_p.wait()
    take_block(1)
    take_mate(0)
    take_mate(1)
    score_half(z // 2)
    take_block(2)
    take_block(3)
    take_mate(2)
    take_mate(3)
    score_half(1 - z // 2)

    def relay(k):
        for q in range(1, nd):
            got = rows_v.at[q, blocks[k]]
            arrive(got, ds_sem.at[0, k], dr_sem.at[q, blocks[k]])
            push(got, got, ds_sem.at[nd + q, k], dr_sem.at[q, blocks[k]], (d, mate))

    my_feats = pl.ds(pl.multiple_of(d * feats, feats), feats)

    def turn(q):
        pt_v[q] = rows_v[q, :, :, my_feats].reshape(rows, feats).T

    def take(q):
        for k in range(half):
            arrive(rows_v.at[q, mates[k]], ds_sem.at[0, k], dr_sem.at[q, mates[k]])
        x = rows_v[q].reshape(rows, width)
        for j in range(0, cols, tile):
            at = slice(j, j + tile)
            scores[q, :, at] = jnp.dot(x, cent_t[:, at], preferred_element_type=jnp.float32) * scale
        turn(q)

    def widen(x):
        return jnp.broadcast_to(x, (LANES, x.shape[1])).T

    step_rows = 32

    def row_stats(q, r, col_potential):
        for g in range(rows // LANES):
            parts = []
            for i in range(g * LANES, (g + 1) * LANES, step_rows):
                xs = []
                for j in range(0, cols, LANES):
                    x = scores[q, i : i + step_rows, j : j + LANES]
                    if col_potential is not None:
                        x = x + col_potential[:, j : j + LANES]
                    xs.append(x)
                m = functools.reduce(jnp.maximum, xs)
                s = functools.reduce(jnp.add, [jnp.exp2(x - m) for x in xs])
                parts.append(m + jnp.log2(s))
            t = jnp.concatenate(parts, axis=0).T
            m = jnp.max(t, axis=0, keepdims=True)
            s = jnp.sum(jnp.exp2(t - m), axis=0, keepdims=True)
            row_slots[r, q, c, :, g * LANES : (g + 1) * LANES] = m + jnp.log2(s)
        mine = row_slots.at[r, q, c]
        for k in range(1, nc):
            push(mine, mine, rs_sem.at[r, q, k], rr_sem.at[r, q, c], (d, lax.rem(c + k, nc)))

    def join(parts):
        peak = functools.reduce(jnp.maximum, parts)
        return peak + jnp.log2(functools.reduce(jnp.add, [jnp.exp2(x - peak) for x in parts]))

    def row_potential(q, r):
        for k in range(1, nc):
            src = lax.rem(c + nc - k, nc)
            arrive(row_slots.at[r, q, src], rs_sem.at[r, q, 0], rr_sem.at[r, q, src])
        return -join([row_slots[r, q, k] for k in range(nc)])

    def col_part(q, r):
        rexp[...] = widen(row_potential(q, r))
        for j in range(0, cols, LANES):
            ms, ss = [], []
            for i in range(0, rows, LANES):
                x = scores[q, i : i + LANES, j : j + LANES] + rexp[i : i + LANES, :]
                x = x.reshape(LANES // 8, 8, LANES)
                m = jnp.max(x, axis=0)
                ms.append(m)
                ss.append(jnp.sum(jnp.exp2(x - m[None]), axis=0))
            m = functools.reduce(jnp.maximum, ms)
            cm[q, :, j : j + LANES] = m
            cs[q, :, j : j + LANES] = functools.reduce(jnp.add, [s * jnp.exp2(a - m) for a, s in zip(ms, ss)])

    def col_merge(n):
        peak = jnp.max(jnp.max(cm[0:n], axis=0), axis=0, keepdims=True)
        total = functools.reduce(jnp.add, [cs[q] * jnp.exp2(cm[q] - peak) for q in range(n)])
        return peak + jnp.log2(jnp.sum(total, axis=0, keepdims=True))

    def split_round(r, col_potential, before, after):
        row_stats(0, r, col_potential)
        before()
        col_part(0, r)
        col_slots[r, 0] = col_merge(1)
        for q in range(1, nd):
            push(col_slots.at[r, 0], col_slots.at[r, q], cs_sem.at[r, q], cr_sem.at[r, q], (docs[q], c))
        after()
        for q in range(1, nd):
            arrive(col_slots.at[r, q], cs_sem.at[r, 0], cr_sem.at[r, q])
        return log_column - join([col_slots[r, q] for q in range(nd)])

    def whole_round(r, col_potential):
        for q in range(nd):
            row_stats(q, r, col_potential)
        for q in range(nd):
            col_part(q, r)
        return log_column - col_merge(nd)

    col_potential = None
    work = [functools.partial(relay, 0), lambda: [relay(k) for k in range(1, half)] + [turn(0)], lambda: [take(1), take(2)], lambda: take(3)]
    for r in range(SPLIT_ROUNDS):
        col_potential = split_round(r, col_potential, *work[2 * r : 2 * r + 2])
    for r in range(SPLIT_ROUNDS, ITERS):
        col_potential = whole_round(r, col_potential)

    for q in range(nd):
        row_stats(q, ITERS, col_potential)
    for q in range(nd):
        rexp[...] = widen(row_slots[ITERS, q, c])
        for j in range(0, cols, LANES):
            at = slice(j, j + LANES)
            e = jnp.exp2(scores[q, :, at] + col_potential[:, at] - rexp[...])
            e_v[q, :, at] = e.astype(jnp.bfloat16)
            if not q:
                own_v[:, at] = e
    pad = lhs.shape[0] - feats
    lane = lax.broadcasted_iota(jnp.int32, (pad, rows), 0)
    for q in range(nd):
        f = jnp.exp2(row_slots[ITERS, q, c] + row_potential(q, ITERS))
        lhs[0:feats, :] = (pt_v[q].astype(jnp.float32) * f).astype(jnp.bfloat16)
        high = f.astype(jnp.bfloat16).astype(jnp.float32)
        lhs[feats:, :] = jnp.where(lane == 0, high, jnp.where(lane == 1, f - high, 0.0)).astype(jnp.bfloat16)
        for j in range(0, cols, tile):
            at = slice(j, j + tile)
            part = jnp.dot(lhs[...], e_v[q, :, at], preferred_element_type=jnp.float32)
            acc_out[:, at] = acc_out[:, at] + part if q else part
        if not q:
            rexp[...] = widen(f * (cols * nc))
            for j in range(0, cols, LANES):
                at = slice(j, j + LANES)
                assign_out[:, at] = (own_v[:, at] * rexp[...]).astype(jnp.bfloat16)
    for copy in sends:
        copy.wait_send()


def finish_kernel(total_rows, total_cols, assign_ref, acc, assign_out, mass_out, newc_out, mass_v, newc_v, out_sem):
    cols = assign_ref.shape[1]
    feats = newc_out.shape[1]
    copies = [pltpu.make_async_copy(assign_ref, assign_out, out_sem.at[0])]
    copies[0].start()
    for j in range(0, cols, LANES):
        at = slice(j, j + LANES)
        mass = acc[feats : feats + 1, at] + acc[feats + 1 : feats + 2, at]
        mass_v[j // LANES : j // LANES + 1, :] = mass * total_cols / total_rows
        newc_v[at, :] = (acc[0:feats, at] / mass).T
        if (j + LANES) % (2 * LANES) == 0:
            part = pl.ds(j - LANES, 2 * LANES)
            copies.append(
                pltpu.make_async_copy(newc_v.at[part], newc_out.at[part], out_sem.at[2 + j // (2 * LANES)])
            )
            copies[-1].start()
    copies.append(pltpu.make_async_copy(mass_v, mass_out, out_sem.at[1]))
    copies[-1].start()
    for copy in copies:
        copy.wait()


def wide_shards(nd, nc, passages, centroids):
    block, width = passages.shape
    cols = centroids.shape[0]
    rows = nc * block
    feats = width // nd
    dma = pltpu.SemaphoreType.DMA
    f32, bf16 = jnp.float32, jnp.bfloat16
    vmem = pl.BlockSpec(memory_space=pltpu.VMEM)
    any_spec = pl.BlockSpec(memory_space=pl.ANY)
    hbm = pltpu.MemorySpace.HBM
    passages, centroids = (pltpu.with_memory_space_constraint(x, hbm) for x in (passages, centroids))
    pad = 16
    assign, acc = pl.pallas_call(
        functools.partial(wide_kernel, nd, nc),
        out_shape=(
            jax.ShapeDtypeStruct((rows, cols), bf16),
            jax.ShapeDtypeStruct((feats + pad, cols), f32),
        ),
        in_specs=[pl.BlockSpec(memory_space=hbm)] * 2,
        out_specs=(vmem,) * 2,
        scratch_shapes=[
            pltpu.VMEM((nd, nc, block, width), bf16),
            pltpu.VMEM((cols, width), bf16),
            pltpu.VMEM((width, cols), bf16),
            pltpu.VMEM((nd, rows, cols), bf16),
            pltpu.VMEM((rows, cols), f32),
            pltpu.VMEM((nd, feats, rows), bf16),
            pltpu.VMEM((feats + pad, rows), bf16),
            pltpu.VMEM((nd, rows, cols), f32),
            pltpu.VMEM((rows, LANES), f32),
            pltpu.VMEM((ITERS + 1, nd, nc, 1, rows), f32),
            pltpu.VMEM((ITERS, nd, 1, cols), f32),
            pltpu.VMEM((nd, 8, cols), f32),
            pltpu.VMEM((nd, 8, cols), f32),
            dma((2,)),
            dma((nc,)),
            dma((nc,)),
            dma((2 * nd, nc // 2)),
            dma((nd, nc)),
            dma((ITERS + 1, nd, nc)),
            dma((ITERS + 1, nd, nc)),
            dma((ITERS, nd)),
            dma((ITERS, nd)),
        ],
        compiler_params=pltpu.CompilerParams(
            collective_id=0, has_side_effects=True, vmem_limit_bytes=44 * 1024 * 1024
        ),
    )(passages, centroids)
    assign, masses, newc = pl.pallas_call(
        functools.partial(finish_kernel, rows * nd, cols * nc),
        out_shape=(
            jax.ShapeDtypeStruct((rows, cols), bf16),
            jax.ShapeDtypeStruct((cols // LANES, LANES), f32),
            jax.ShapeDtypeStruct((cols, feats), f32),
        ),
        in_specs=[vmem] * 2,
        out_specs=(any_spec,) * 3,
        scratch_shapes=[
            pltpu.VMEM((cols // LANES, LANES), f32),
            pltpu.VMEM((cols, feats), f32),
            dma((2 + cols // (2 * LANES),)),
        ],
        compiler_params=pltpu.CompilerParams(vmem_limit_bytes=32 * 1024 * 1024),
    )(assign, acc)
    return assign, masses.reshape(cols), newc


def shards(nd, nc, passages, centroids):
    block, width = passages.shape
    cols = centroids.shape[0]
    rows = nc * block
    feats = width // nd
    if nd == 4 and nc == 8 and nd * rows * cols <= 2**21 and rows % LANES == 0 and cols % 256 == 0:
        return wide_shards(nd, nc, passages, centroids)
    any_spec = pl.BlockSpec(memory_space=pl.ANY)
    dma = pltpu.SemaphoreType.DMA
    f32, bf16 = jnp.float32, jnp.bfloat16
    assign, masses, newc = pl.pallas_call(
        functools.partial(kernel, nd, nc),
        out_shape=(
            jax.ShapeDtypeStruct((rows, cols), bf16),
            jax.ShapeDtypeStruct((1, cols), f32),
            jax.ShapeDtypeStruct((cols, feats), f32),
        ),
        in_specs=[pl.BlockSpec(memory_space=pltpu.MemorySpace.HBM)] * 2,
        out_specs=(any_spec, pl.BlockSpec(memory_space=pltpu.VMEM), any_spec),
        scratch_shapes=[
            pltpu.VMEM((nc, block, width), bf16),
            pltpu.VMEM((cols, width), bf16),
            pltpu.VMEM((rows, cols), f32),
            pltpu.VMEM((rows, LANES), f32),
            pltpu.VMEM((rows, LANES), f32),
            pltpu.VMEM((ITERS + 1, nc, 2, rows), f32),
            pltpu.VMEM((ITERS, nd, 2, cols), f32),
            pltpu.VMEM((nd, 1, cols), f32),
            pltpu.VMEM((rows, cols), bf16),
            pltpu.VMEM((nd, cols, feats), bf16),
            pltpu.VMEM((nd, cols, feats), bf16),
            pltpu.VMEM((cols, feats), f32),
            dma((2,)),
            dma((nc,)),
            dma((nc,)),
            dma((ITERS + 1, nc)),
            dma((ITERS + 1, nc)),
            dma((ITERS, nd)),
            dma((ITERS, nd)),
            dma((nd,)),
            dma((nd,)),
            dma((nd,)),
            dma((nd,)),
            dma((2,)),
        ],
        compiler_params=pltpu.CompilerParams(
            collective_id=0, has_side_effects=True, vmem_limit_bytes=52 * 1024 * 1024
        ),
    )(passages, centroids)
    return assign, masses.reshape(cols), newc


def solution(mesh):
    nd, nc = mesh.shape["doc"], mesh.shape["cen"]
    in_specs = (P(("doc", "cen"), None), P("cen", None))
    out_specs = (P("doc", "cen"), P("cen"), P("cen", "doc"))
    return jax.shard_map(
        functools.partial(shards, nd, nc), mesh=mesh, in_specs=in_specs, out_specs=out_specs, check_vma=False
    )
```

```python
import functools
import math

import jax
import jax.numpy as jnp
from jax import lax
from jax.experimental import pallas as pl
from jax.experimental.pallas import tpu as pltpu
from jax.sharding import PartitionSpec as P

ITERS = 3
MESH = pl.DeviceIdType.MESH
LANES = 128


def kernel(
    nd, nc, p_ref, c_ref, assign_out, mass_out, newc_out,
    rows_v, cent_v, scores, rp_v, tbuf, row_slots, col_slots, mass_slots, assign_v, part_send, part_recv, newc_v,
    load_sem, gs_sem, gr_sem, rs_sem, rr_sem, cs_sem, cr_sem, ms_sem, mr_sem, ps_sem, pr_sem, out_sem,
):
    d = lax.axis_index("doc")
    c = lax.axis_index("cen")
    block, width = p_ref.shape
    cols = c_ref.shape[0]
    rows = nc * block
    feats = width // nd
    total_cols = cols * nc
    total_rows = rows * nd
    scale = 1.0 / math.sqrt(width)
    log_column = math.log(total_rows / total_cols)
    sends = []

    load_p = pltpu.make_async_copy(p_ref, rows_v.at[c], load_sem.at[0])
    load_c = pltpu.make_async_copy(c_ref, cent_v, load_sem.at[1])
    load_p.start()
    load_c.start()

    barrier = pltpu.get_barrier_semaphore()
    for k in range(1, nc):
        pl.semaphore_signal(barrier, inc=1, device_id=(d, lax.rem(c + k, nc)), device_id_type=MESH)
    for k in range(1, nd):
        pl.semaphore_signal(barrier, inc=1, device_id=(lax.rem(d + k, nd), c), device_id_type=MESH)
    pl.semaphore_wait(barrier, nc + nd - 2)
    load_p.wait()

    def push(src, dst, send, recv, where):
        copy = pltpu.make_async_remote_copy(
            src_ref=src, dst_ref=dst, send_sem=send, recv_sem=recv, device_id=where, device_id_type=MESH
        )
        copy.start()
        sends.append(copy)

    def arrive(ref, send, recv):
        pltpu.make_async_remote_copy(
            src_ref=ref, dst_ref=ref, send_sem=send, recv_sem=recv, device_id=(d, c), device_id_type=MESH
        ).wait_recv()

    mate = c + 1 - 2 * lax.rem(c, 2)
    half = nc // 2
    for k in range(1, half):
        push(rows_v.at[c], rows_v.at[c], gs_sem.at[k], gr_sem.at[c], (d, lax.rem(c + 2 * k, nc)))
    push(rows_v.at[c], rows_v.at[c], gs_sem.at[0], gr_sem.at[c], (d, mate))
    order = [k for pair in zip(range(1, half), reversed(range(1, half))) for k in pair][: half - 1]
    for k in order:
        src = lax.rem(c + nc - 2 * k, nc)
        arrive(rows_v.at[src], gs_sem.at[half + k], gr_sem.at[src])
        push(rows_v.at[src], rows_v.at[src], gs_sem.at[half + k], gr_sem.at[src], (d, mate))
    arrive(rows_v.at[mate], gs_sem.at[0], gr_sem.at[mate])
    for k in range(1, half):
        src = lax.rem(mate + nc - 2 * k, nc)
        arrive(rows_v.at[src], gs_sem.at[0], gr_sem.at[src])
    load_c.wait()

    group_rows = rows_v[...].reshape(rows, width)
    tile = min(256, cols)
    for j in range(cols // tile):
        at = slice(j * tile, (j + 1) * tile)
        scores[:, at] = (
            lax.dot_general(
                group_rows, cent_v[at, :], (((1,), (1,)), ((), ())), preferred_element_type=jnp.float32
            )
            * scale
        )

    step_rows = 64
    lane = lax.broadcasted_iota(jnp.int32, (step_rows, LANES), 1)

    def combine(slots, r, n):
        peak = slots[r, 0, 0:1, :]
        for k in range(1, n):
            peak = jnp.maximum(peak, slots[r, k, 0:1, :])
        total = jnp.zeros_like(peak)
        for k in range(n):
            total = total + slots[r, k, 1:2, :] * jnp.exp(slots[r, k, 0:1, :] - peak)
        return peak + jnp.log(total)

    def row_round(r, col_potential):
        @pl.loop(0, rows // step_rows)
        def _(i):
            at = pl.ds(pl.multiple_of(i * step_rows, step_rows), step_rows)
            x = scores[at, :]
            if col_potential is not None:
                x = x + col_potential
            m = jnp.max(x, axis=1, keepdims=True)
            s = jnp.sum(jnp.exp(x - m), axis=1, keepdims=True)
            tbuf[at, :] = jnp.where(lane == 0, m, s)

        row_slots[r, c, :, :] = tbuf[...].T[0:2, :]
        for k in range(1, nc):
            push(row_slots.at[r, c], row_slots.at[r, c], rs_sem.at[r, k], rr_sem.at[r, c], (d, lax.rem(c + k, nc)))
        for k in range(1, nc):
            src = lax.rem(c + nc - k, nc)
            arrive(row_slots.at[r, src], rs_sem.at[r, k], rr_sem.at[r, src])
        row_potential = -combine(row_slots, r, nc)
        rp_v[...] = jnp.broadcast_to(row_potential, (LANES, rows)).T

    def col_round(r):
        for j in range(cols // LANES):
            at = slice(j * LANES, (j + 1) * LANES)
            x = scores[:, at] + rp_v[...]
            m = jnp.max(x, axis=0, keepdims=True)
            s = jnp.sum(jnp.exp(x - m), axis=0, keepdims=True)
            col_slots[r, d, 0:1, at] = m
            col_slots[r, d, 1:2, at] = s
        for k in range(1, nd):
            push(col_slots.at[r, d], col_slots.at[r, d], cs_sem.at[r, k], cr_sem.at[r, d], (lax.rem(d + k, nd), c))
        for k in range(1, nd):
            src = lax.rem(d + nd - k, nd)
            arrive(col_slots.at[r, src], cs_sem.at[r, k], cr_sem.at[r, src])
        return log_column - combine(col_slots, r, nd)

    col_potential = None
    for r in range(ITERS):
        row_round(r, col_potential)
        col_potential = col_round(r)
    row_round(ITERS, col_potential)

    for j in range(cols // LANES):
        at = slice(j * LANES, (j + 1) * LANES)
        w = jnp.exp(scores[:, at] + rp_v[...] + col_potential[:, at])
        mass_slots[d, :, at] = jnp.sum(w, axis=0, keepdims=True)
        assign_v[:, at] = (w * total_cols).astype(jnp.bfloat16)
    assign_copy = pltpu.make_async_copy(assign_v, assign_out, out_sem.at[0])
    assign_copy.start()
    for k in range(1, nd):
        push(mass_slots.at[d], mass_slots.at[d], ms_sem.at[k], mr_sem.at[d], (lax.rem(d + k, nd), c))

    def partial(q):
        r3 = rows_v[:, :, pl.ds(pl.multiple_of(q * feats, feats), feats)].reshape(rows, feats)
        return lax.dot_general(
            assign_v[...], r3, (((0,), (0,)), ((), ())), preferred_element_type=jnp.float32
        ).astype(jnp.bfloat16)

    for k in reversed(range(1, nd)):
        q = lax.rem(d + k, nd)
        part_send[k, :, :] = partial(q)
        push(part_send.at[k], part_recv.at[d], ps_sem.at[k], pr_sem.at[d], (q, c))
    part_recv[d, :, :] = partial(d)

    for k in range(1, nd):
        src = lax.rem(d + nd - k, nd)
        arrive(mass_slots.at[src], ms_sem.at[k], mr_sem.at[src])
    raw_mass = mass_slots[0]
    for k in range(1, nd):
        raw_mass = raw_mass + mass_slots[k]
    mass_out[...] = raw_mass * total_cols / total_rows
    mass_col = jnp.broadcast_to(raw_mass, (LANES, cols)).T

    for k in range(1, nd):
        src = lax.rem(d + nd - k, nd)
        arrive(part_recv.at[src], ps_sem.at[k], pr_sem.at[src])
    for j in range(feats // LANES):
        at = slice(j * LANES, (j + 1) * LANES)
        sums = part_recv[0, :, at].astype(jnp.float32)
        for k in range(1, nd):
            sums = sums + part_recv[k, :, at].astype(jnp.float32)
        newc_v[:, at] = sums / total_cols / mass_col
    newc_copy = pltpu.make_async_copy(newc_v, newc_out, out_sem.at[1])
    newc_copy.start()
    for copy in sends:
        copy.wait_send()
    assign_copy.wait()
    newc_copy.wait()


SPLIT_ROUNDS = 2


def wide_kernel(
    nd, nc, p_ref, c_ref, assign_out, acc_out,
    rows_v, cent_v, cent_t, e_v, own_v, pt_v, lhs, scores, rexp, row_slots, col_slots, cm, cs,
    load_sem, gs_sem, gr_sem, ds_sem, dr_sem, rs_sem, rr_sem, cs_sem, cr_sem,
):
    d = lax.axis_index("doc")
    c = lax.axis_index("cen")
    block, width = p_ref.shape
    cols = c_ref.shape[0]
    rows = nc * block
    feats = width // nd
    scale = math.log2(math.e) / math.sqrt(width)
    log_column = math.log2(rows * nd / (cols * nc))
    sends = []
    mate = c + 1 - 2 * lax.rem(c, 2)
    half = nc // 2
    beside = d + 1 - 2 * lax.rem(d, 2)
    docs = [d, beside, lax.rem(d + 2, nd), lax.rem(beside + 2, nd)]

    barrier = pltpu.get_barrier_semaphore()
    for k in range(1, nc):
        pl.semaphore_signal(barrier, inc=1, device_id=(d, lax.rem(c + k, nc)), device_id_type=MESH)
    for q in range(1, nd):
        pl.semaphore_signal(barrier, inc=1, device_id=(docs[q], c), device_id_type=MESH)
    load_p = pltpu.make_async_copy(p_ref, rows_v.at[0, c], load_sem.at[0])
    load_c = pltpu.make_async_copy(c_ref, cent_v, load_sem.at[1])
    load_p.start()
    load_c.start()
    pl.semaphore_wait(barrier, nc + nd - 2)

    def push(src, dst, send, recv, where):
        copy = pltpu.make_async_remote_copy(
            src_ref=src, dst_ref=dst, send_sem=send, recv_sem=recv, device_id=where, device_id_type=MESH
        )
        copy.start()
        sends.append(copy)

    def arrive(ref, send, recv):
        pltpu.make_async_remote_copy(
            src_ref=ref, dst_ref=ref, send_sem=send, recv_sem=recv, device_id=(d, c), device_id_type=MESH
        ).wait_recv()

    z = c // 2
    near = c + 2 - 4 * lax.rem(z, 2)
    blocks = [c, near, lax.rem(c + half, nc), lax.rem(near + half, nc)]
    mates = [b + mate - c for b in blocks]
    tile = min(256, cols)

    def to_docs(src, k):
        for q in range(1, nd):
            push(src, rows_v.at[q, blocks[k]], ds_sem.at[q, k], dr_sem.at[q, blocks[k]], (docs[q], c))

    def take_block(k):
        got = rows_v.at[0, blocks[k]]
        arrive(got, gs_sem.at[half + k], gr_sem.at[blocks[k]])
        push(got, got, gs_sem.at[half + k], gr_sem.at[blocks[k]], (d, mate))
        if k < half - 1:
            to_docs(got, k)

    def take_mate(k):
        arrive(rows_v.at[0, mates[k]], gs_sem.at[0], gr_sem.at[mates[k]])

    def score_half(h):
        x = rows_v[0, pl.ds(h * half, half)].reshape(rows // 2, width)
        to = pl.ds(pl.multiple_of(h * (rows // 2), 32), rows // 2)
        for j in range(0, cols, tile):
            at = slice(j, j + tile)
            scores[0, to, at] = jnp.dot(x, cent_t[:, at], preferred_element_type=jnp.float32) * scale

    for k in range(1, half):
        push(p_ref, rows_v.at[0, c], gs_sem.at[k], gr_sem.at[c], (d, blocks[k]))
    push(p_ref, rows_v.at[0, c], gs_sem.at[0], gr_sem.at[c], (d, mate))
    to_docs(p_ref, 0)
    load_c.wait()
    cent_t[...] = cent_v[...].T
    load_p.wait()
    take_block(1)
    take_mate(0)
    take_mate(1)
    score_half(z // 2)
    take_block(2)
    take_block(3)
    take_mate(2)
    take_mate(3)
    score_half(1 - z // 2)

    def relay(k):
        for q in range(1, nd):
            got = rows_v.at[q, blocks[k]]
            arrive(got, ds_sem.at[0, k], dr_sem.at[q, blocks[k]])
            push(got, got, ds_sem.at[nd + q, k], dr_sem.at[q, blocks[k]], (d, mate))

    my_feats = pl.ds(pl.multiple_of(d * feats, feats), feats)

    def turn(q):
        pt_v[q] = rows_v[q, :, :, my_feats].reshape(rows, feats).T

    def take(q):
        for k in range(half):
            arrive(rows_v.at[q, mates[k]], ds_sem.at[0, k], dr_sem.at[q, mates[k]])
        x = rows_v[q].reshape(rows, width)
        for j in range(0, cols, tile):
            at = slice(j, j + tile)
            scores[q, :, at] = jnp.dot(x, cent_t[:, at], preferred_element_type=jnp.float32) * scale
        turn(q)

    def widen(x):
        return jnp.broadcast_to(x, (LANES, x.shape[1])).T

    step_rows = 32

    def row_stats(q, r, col_potential):
        for g in range(rows // LANES):
            parts = []
            for i in range(g * LANES, (g + 1) * LANES, step_rows):
                xs = []
                for j in range(0, cols, LANES):
                    x = scores[q, i : i + step_rows, j : j + LANES]
                    if col_potential is not None:
                        x = x + col_potential[:, j : j + LANES]
                    xs.append(x)
                m = functools.reduce(jnp.maximum, xs)
                s = functools.reduce(jnp.add, [jnp.exp2(x - m) for x in xs])
                parts.append(m + jnp.log2(s))
            t = jnp.concatenate(parts, axis=0).T
            m = jnp.max(t, axis=0, keepdims=True)
            s = jnp.sum(jnp.exp2(t - m), axis=0, keepdims=True)
            row_slots[r, q, c, :, g * LANES : (g + 1) * LANES] = m + jnp.log2(s)
        mine = row_slots.at[r, q, c]
        for k in range(1, nc):
            push(mine, mine, rs_sem.at[r, q, k], rr_sem.at[r, q, c], (d, lax.rem(c + k, nc)))

    def join(parts):
        peak = functools.reduce(jnp.maximum, parts)
        return peak + jnp.log2(functools.reduce(jnp.add, [jnp.exp2(x - peak) for x in parts]))

    def row_potential(q, r):
        for k in range(1, nc):
            src = lax.rem(c + nc - k, nc)
            arrive(row_slots.at[r, q, src], rs_sem.at[r, q, 0], rr_sem.at[r, q, src])
        return -join([row_slots[r, q, k] for k in range(nc)])

    def col_part(q, r):
        rexp[...] = widen(row_potential(q, r))
        for j in range(0, cols, LANES):
            ms, ss = [], []
            for i in range(0, rows, LANES):
                x = scores[q, i : i + LANES, j : j + LANES] + rexp[i : i + LANES, :]
                x = x.reshape(LANES // 8, 8, LANES)
                m = jnp.max(x, axis=0)
                ms.append(m)
                ss.append(jnp.sum(jnp.exp2(x - m[None]), axis=0))
            m = functools.reduce(jnp.maximum, ms)
            cm[q, :, j : j + LANES] = m
            cs[q, :, j : j + LANES] = functools.reduce(jnp.add, [s * jnp.exp2(a - m) for a, s in zip(ms, ss)])

    def col_merge(n):
        peak = jnp.max(jnp.max(cm[0:n], axis=0), axis=0, keepdims=True)
        total = functools.reduce(jnp.add, [cs[q] * jnp.exp2(cm[q] - peak) for q in range(n)])
        return peak + jnp.log2(jnp.sum(total, axis=0, keepdims=True))

    def split_round(r, col_potential, before, after):
        row_stats(0, r, col_potential)
        before()
        col_part(0, r)
        col_slots[r, 0] = col_merge(1)
        for q in range(1, nd):
            push(col_slots.at[r, 0], col_slots.at[r, q], cs_sem.at[r, q], cr_sem.at[r, q], (docs[q], c))
        after()
        for q in range(1, nd):
            arrive(col_slots.at[r, q], cs_sem.at[r, 0], cr_sem.at[r, q])
        return log_column - join([col_slots[r, q] for q in range(nd)])

    def whole_round(r, col_potential):
        for q in range(nd):
            row_stats(q, r, col_potential)
        for q in range(nd):
            col_part(q, r)
        return log_column - col_merge(nd)

    col_potential = None
    plan = [[(0, 0), (0, 1)], [(3, 3), (2, 0)], [(0, 2), (0, 3)], [(1, 1), (1, 2), (1, 3)]]
    jobs = {0: relay, 1: take, 2: turn, 3: lambda k: to_docs(rows_v.at[0, blocks[k]], k)}
    work = [lambda todo=todo: [jobs[a](b) for a, b in todo] for todo in plan]
    for r in range(SPLIT_ROUNDS):
        col_potential = split_round(r, col_potential, *work[2 * r : 2 * r + 2])
    for r in range(SPLIT_ROUNDS, ITERS):
        col_potential = whole_round(r, col_potential)

    for q in range(nd):
        row_stats(q, ITERS, col_potential)
    for q in range(nd):
        rexp[...] = widen(row_slots[ITERS, q, c])
        for j in range(0, cols, LANES):
            at = slice(j, j + LANES)
            e = jnp.exp2(scores[q, :, at] + col_potential[:, at] - rexp[...])
            e_v[q, :, at] = e.astype(jnp.bfloat16)
            if not q:
                own_v[:, at] = e
    pad = lhs.shape[0] - feats
    lane = lax.broadcasted_iota(jnp.int32, (pad, rows), 0)
    for q in range(nd):
        f = jnp.exp2(row_slots[ITERS, q, c] + row_potential(q, ITERS))
        lhs[0:feats, :] = (pt_v[q].astype(jnp.float32) * f).astype(jnp.bfloat16)
        high = f.astype(jnp.bfloat16).astype(jnp.float32)
        lhs[feats:, :] = jnp.where(lane == 0, high, jnp.where(lane == 1, f - high, 0.0)).astype(jnp.bfloat16)
        for j in range(0, cols, tile):
            at = slice(j, j + tile)
            part = jnp.dot(lhs[...], e_v[q, :, at], preferred_element_type=jnp.float32)
            acc_out[:, at] = acc_out[:, at] + part if q else part
        if not q:
            rexp[...] = widen(f * (cols * nc))
            for j in range(0, cols, LANES):
                at = slice(j, j + LANES)
                assign_out[:, at] = (own_v[:, at] * rexp[...]).astype(jnp.bfloat16)
    for copy in sends:
        copy.wait_send()


def finish_kernel(total_rows, total_cols, assign_ref, acc, assign_out, mass_out, newc_out, mass_v, newc_v, out_sem):
    cols = assign_ref.shape[1]
    feats = newc_out.shape[1]
    copies = [pltpu.make_async_copy(assign_ref, assign_out, out_sem.at[0])]
    copies[0].start()
    for j in range(0, cols, LANES):
        at = slice(j, j + LANES)
        mass = acc[feats : feats + 1, at] + acc[feats + 1 : feats + 2, at]
        mass_v[j // LANES : j // LANES + 1, :] = mass * total_cols / total_rows
        newc_v[at, :] = (acc[0:feats, at] / mass).T
        if (j + LANES) % (2 * LANES) == 0:
            part = pl.ds(j - LANES, 2 * LANES)
            copies.append(
                pltpu.make_async_copy(newc_v.at[part], newc_out.at[part], out_sem.at[2 + j // (2 * LANES)])
            )
            copies[-1].start()
    copies.append(pltpu.make_async_copy(mass_v, mass_out, out_sem.at[1]))
    copies[-1].start()
    for copy in copies:
        copy.wait()


def wide_shards(nd, nc, passages, centroids):
    block, width = passages.shape
    cols = centroids.shape[0]
    rows = nc * block
    feats = width // nd
    dma = pltpu.SemaphoreType.DMA
    f32, bf16 = jnp.float32, jnp.bfloat16
    vmem = pl.BlockSpec(memory_space=pltpu.VMEM)
    any_spec = pl.BlockSpec(memory_space=pl.ANY)
    hbm = pltpu.MemorySpace.HBM
    passages, centroids = (pltpu.with_memory_space_constraint(x, hbm) for x in (passages, centroids))
    pad = 16
    assign, acc = pl.pallas_call(
        functools.partial(wide_kernel, nd, nc),
        out_shape=(
            jax.ShapeDtypeStruct((rows, cols), bf16),
            jax.ShapeDtypeStruct((feats + pad, cols), f32),
        ),
        in_specs=[pl.BlockSpec(memory_space=hbm)] * 2,
        out_specs=(vmem,) * 2,
        scratch_shapes=[
            pltpu.VMEM((nd, nc, block, width), bf16),
            pltpu.VMEM((cols, width), bf16),
            pltpu.VMEM((width, cols), bf16),
            pltpu.VMEM((nd, rows, cols), bf16),
            pltpu.VMEM((rows, cols), f32),
            pltpu.VMEM((nd, feats, rows), bf16),
            pltpu.VMEM((feats + pad, rows), bf16),
            pltpu.VMEM((nd, rows, cols), f32),
            pltpu.VMEM((rows, LANES), f32),
            pltpu.VMEM((ITERS + 1, nd, nc, 1, rows), f32),
            pltpu.VMEM((ITERS, nd, 1, cols), f32),
            pltpu.VMEM((nd, 8, cols), f32),
            pltpu.VMEM((nd, 8, cols), f32),
            dma((2,)),
            dma((nc,)),
            dma((nc,)),
            dma((2 * nd, nc // 2)),
            dma((nd, nc)),
            dma((ITERS + 1, nd, nc)),
            dma((ITERS + 1, nd, nc)),
            dma((ITERS, nd)),
            dma((ITERS, nd)),
        ],
        compiler_params=pltpu.CompilerParams(
            collective_id=0, has_side_effects=True, vmem_limit_bytes=44 * 1024 * 1024
        ),
    )(passages, centroids)
    assign, masses, newc = pl.pallas_call(
        functools.partial(finish_kernel, rows * nd, cols * nc),
        out_shape=(
            jax.ShapeDtypeStruct((rows, cols), bf16),
            jax.ShapeDtypeStruct((cols // LANES, LANES), f32),
            jax.ShapeDtypeStruct((cols, feats), f32),
        ),
        in_specs=[vmem] * 2,
        out_specs=(any_spec,) * 3,
        scratch_shapes=[
            pltpu.VMEM((cols // LANES, LANES), f32),
            pltpu.VMEM((cols, feats), f32),
            dma((2 + cols // (2 * LANES),)),
        ],
        compiler_params=pltpu.CompilerParams(vmem_limit_bytes=32 * 1024 * 1024),
    )(assign, acc)
    return assign, masses.reshape(cols), newc


def shards(nd, nc, passages, centroids):
    block, width = passages.shape
    cols = centroids.shape[0]
    rows = nc * block
    feats = width // nd
    if nd == 4 and nc == 8 and nd * rows * cols <= 2**21 and rows % LANES == 0 and cols % 256 == 0:
        return wide_shards(nd, nc, passages, centroids)
    any_spec = pl.BlockSpec(memory_space=pl.ANY)
    dma = pltpu.SemaphoreType.DMA
    f32, bf16 = jnp.float32, jnp.bfloat16
    assign, masses, newc = pl.pallas_call(
        functools.partial(kernel, nd, nc),
        out_shape=(
            jax.ShapeDtypeStruct((rows, cols), bf16),
            jax.ShapeDtypeStruct((1, cols), f32),
            jax.ShapeDtypeStruct((cols, feats), f32),
        ),
        in_specs=[pl.BlockSpec(memory_space=pltpu.MemorySpace.HBM)] * 2,
        out_specs=(any_spec, pl.BlockSpec(memory_space=pltpu.VMEM), any_spec),
        scratch_shapes=[
            pltpu.VMEM((nc, block, width), bf16),
            pltpu.VMEM((cols, width), bf16),
            pltpu.VMEM((rows, cols), f32),
            pltpu.VMEM((rows, LANES), f32),
            pltpu.VMEM((rows, LANES), f32),
            pltpu.VMEM((ITERS + 1, nc, 2, rows), f32),
            pltpu.VMEM((ITERS, nd, 2, cols), f32),
            pltpu.VMEM((nd, 1, cols), f32),
            pltpu.VMEM((rows, cols), bf16),
            pltpu.VMEM((nd, cols, feats), bf16),
            pltpu.VMEM((nd, cols, feats), bf16),
            pltpu.VMEM((cols, feats), f32),
            dma((2,)),
            dma((nc,)),
            dma((nc,)),
            dma((ITERS + 1, nc)),
            dma((ITERS + 1, nc)),
            dma((ITERS, nd)),
            dma((ITERS, nd)),
            dma((nd,)),
            dma((nd,)),
            dma((nd,)),
            dma((nd,)),
            dma((2,)),
        ],
        compiler_params=pltpu.CompilerParams(
            collective_id=0, has_side_effects=True, vmem_limit_bytes=52 * 1024 * 1024
        ),
    )(passages, centroids)
    return assign, masses.reshape(cols), newc


def solution(mesh):
    nd, nc = mesh.shape["doc"], mesh.shape["cen"]
    in_specs = (P(("doc", "cen"), None), P("cen", None))
    out_specs = (P("doc", "cen"), P("cen"), P("cen", "doc"))
    return jax.shard_map(
        functools.partial(shards, nd, nc), mesh=mesh, in_specs=in_specs, out_specs=out_specs, check_vma=False
    )
```

```python
import functools
import math

import jax
import jax.numpy as jnp
from jax import lax
from jax.experimental import pallas as pl
from jax.experimental.pallas import tpu as pltpu
from jax.sharding import PartitionSpec as P

ITERS = 3
MESH = pl.DeviceIdType.MESH
LANES = 128


def kernel(
    nd, nc, p_ref, c_ref, assign_out, mass_out, newc_out,
    rows_v, cent_v, scores, rp_v, tbuf, row_slots, col_slots, mass_slots, assign_v, part_send, part_recv, newc_v,
    load_sem, gs_sem, gr_sem, rs_sem, rr_sem, cs_sem, cr_sem, ms_sem, mr_sem, ps_sem, pr_sem, out_sem,
):
    d = lax.axis_index("doc")
    c = lax.axis_index("cen")
    block, width = p_ref.shape
    cols = c_ref.shape[0]
    rows = nc * block
    feats = width // nd
    total_cols = cols * nc
    total_rows = rows * nd
    scale = 1.0 / math.sqrt(width)
    log_column = math.log(total_rows / total_cols)
    sends = []

    load_p = pltpu.make_async_copy(p_ref, rows_v.at[c], load_sem.at[0])
    load_c = pltpu.make_async_copy(c_ref, cent_v, load_sem.at[1])
    load_p.start()
    load_c.start()

    barrier = pltpu.get_barrier_semaphore()
    for k in range(1, nc):
        pl.semaphore_signal(barrier, inc=1, device_id=(d, lax.rem(c + k, nc)), device_id_type=MESH)
    for k in range(1, nd):
        pl.semaphore_signal(barrier, inc=1, device_id=(lax.rem(d + k, nd), c), device_id_type=MESH)
    pl.semaphore_wait(barrier, nc + nd - 2)
    load_p.wait()

    def push(src, dst, send, recv, where):
        copy = pltpu.make_async_remote_copy(
            src_ref=src, dst_ref=dst, send_sem=send, recv_sem=recv, device_id=where, device_id_type=MESH
        )
        copy.start()
        sends.append(copy)

    def arrive(ref, send, recv):
        pltpu.make_async_remote_copy(
            src_ref=ref, dst_ref=ref, send_sem=send, recv_sem=recv, device_id=(d, c), device_id_type=MESH
        ).wait_recv()

    mate = c + 1 - 2 * lax.rem(c, 2)
    half = nc // 2
    for k in range(1, half):
        push(rows_v.at[c], rows_v.at[c], gs_sem.at[k], gr_sem.at[c], (d, lax.rem(c + 2 * k, nc)))
    push(rows_v.at[c], rows_v.at[c], gs_sem.at[0], gr_sem.at[c], (d, mate))
    order = [k for pair in zip(range(1, half), reversed(range(1, half))) for k in pair][: half - 1]
    for k in order:
        src = lax.rem(c + nc - 2 * k, nc)
        arrive(rows_v.at[src], gs_sem.at[half + k], gr_sem.at[src])
        push(rows_v.at[src], rows_v.at[src], gs_sem.at[half + k], gr_sem.at[src], (d, mate))
    arrive(rows_v.at[mate], gs_sem.at[0], gr_sem.at[mate])
    for k in range(1, half):
        src = lax.rem(mate + nc - 2 * k, nc)
        arrive(rows_v.at[src], gs_sem.at[0], gr_sem.at[src])
    load_c.wait()

    group_rows = rows_v[...].reshape(rows, width)
    tile = min(256, cols)
    for j in range(cols // tile):
        at = slice(j * tile, (j + 1) * tile)
        scores[:, at] = (
            lax.dot_general(
                group_rows, cent_v[at, :], (((1,), (1,)), ((), ())), preferred_element_type=jnp.float32
            )
            * scale
        )

    step_rows = 64
    lane = lax.broadcasted_iota(jnp.int32, (step_rows, LANES), 1)

    def combine(slots, r, n):
        peak = slots[r, 0, 0:1, :]
        for k in range(1, n):
            peak = jnp.maximum(peak, slots[r, k, 0:1, :])
        total = jnp.zeros_like(peak)
        for k in range(n):
            total = total + slots[r, k, 1:2, :] * jnp.exp(slots[r, k, 0:1, :] - peak)
        return peak + jnp.log(total)

    def row_round(r, col_potential):
        @pl.loop(0, rows // step_rows)
        def _(i):
            at = pl.ds(pl.multiple_of(i * step_rows, step_rows), step_rows)
            x = scores[at, :]
            if col_potential is not None:
                x = x + col_potential
            m = jnp.max(x, axis=1, keepdims=True)
            s = jnp.sum(jnp.exp(x - m), axis=1, keepdims=True)
            tbuf[at, :] = jnp.where(lane == 0, m, s)

        row_slots[r, c, :, :] = tbuf[...].T[0:2, :]
        for k in range(1, nc):
            push(row_slots.at[r, c], row_slots.at[r, c], rs_sem.at[r, k], rr_sem.at[r, c], (d, lax.rem(c + k, nc)))
        for k in range(1, nc):
            src = lax.rem(c + nc - k, nc)
            arrive(row_slots.at[r, src], rs_sem.at[r, k], rr_sem.at[r, src])
        row_potential = -combine(row_slots, r, nc)
        rp_v[...] = jnp.broadcast_to(row_potential, (LANES, rows)).T

    def col_round(r):
        for j in range(cols // LANES):
            at = slice(j * LANES, (j + 1) * LANES)
            x = scores[:, at] + rp_v[...]
            m = jnp.max(x, axis=0, keepdims=True)
            s = jnp.sum(jnp.exp(x - m), axis=0, keepdims=True)
            col_slots[r, d, 0:1, at] = m
            col_slots[r, d, 1:2, at] = s
        for k in range(1, nd):
            push(col_slots.at[r, d], col_slots.at[r, d], cs_sem.at[r, k], cr_sem.at[r, d], (lax.rem(d + k, nd), c))
        for k in range(1, nd):
            src = lax.rem(d + nd - k, nd)
            arrive(col_slots.at[r, src], cs_sem.at[r, k], cr_sem.at[r, src])
        return log_column - combine(col_slots, r, nd)

    col_potential = None
    for r in range(ITERS):
        row_round(r, col_potential)
        col_potential = col_round(r)
    row_round(ITERS, col_potential)

    for j in range(cols // LANES):
        at = slice(j * LANES, (j + 1) * LANES)
        w = jnp.exp(scores[:, at] + rp_v[...] + col_potential[:, at])
        mass_slots[d, :, at] = jnp.sum(w, axis=0, keepdims=True)
        assign_v[:, at] = (w * total_cols).astype(jnp.bfloat16)
    assign_copy = pltpu.make_async_copy(assign_v, assign_out, out_sem.at[0])
    assign_copy.start()
    for k in range(1, nd):
        push(mass_slots.at[d], mass_slots.at[d], ms_sem.at[k], mr_sem.at[d], (lax.rem(d + k, nd), c))

    def partial(q):
        r3 = rows_v[:, :, pl.ds(pl.multiple_of(q * feats, feats), feats)].reshape(rows, feats)
        return lax.dot_general(
            assign_v[...], r3, (((0,), (0,)), ((), ())), preferred_element_type=jnp.float32
        ).astype(jnp.bfloat16)

    for k in reversed(range(1, nd)):
        q = lax.rem(d + k, nd)
        part_send[k, :, :] = partial(q)
        push(part_send.at[k], part_recv.at[d], ps_sem.at[k], pr_sem.at[d], (q, c))
    part_recv[d, :, :] = partial(d)

    for k in range(1, nd):
        src = lax.rem(d + nd - k, nd)
        arrive(mass_slots.at[src], ms_sem.at[k], mr_sem.at[src])
    raw_mass = mass_slots[0]
    for k in range(1, nd):
        raw_mass = raw_mass + mass_slots[k]
    mass_out[...] = raw_mass * total_cols / total_rows
    mass_col = jnp.broadcast_to(raw_mass, (LANES, cols)).T

    for k in range(1, nd):
        src = lax.rem(d + nd - k, nd)
        arrive(part_recv.at[src], ps_sem.at[k], pr_sem.at[src])
    for j in range(feats // LANES):
        at = slice(j * LANES, (j + 1) * LANES)
        sums = part_recv[0, :, at].astype(jnp.float32)
        for k in range(1, nd):
            sums = sums + part_recv[k, :, at].astype(jnp.float32)
        newc_v[:, at] = sums / total_cols / mass_col
    newc_copy = pltpu.make_async_copy(newc_v, newc_out, out_sem.at[1])
    newc_copy.start()
    for copy in sends:
        copy.wait_send()
    assign_copy.wait()
    newc_copy.wait()


SPLIT_ROUNDS = 2


def wide_kernel(
    nd, nc, p_ref, c_ref, assign_out, acc_out,
    rows_v, cent_v, cent_t, e_v, own_v, pt_v, lhs, scores, rexp, row_slots, col_slots, cm, cs,
    load_sem, gs_sem, gr_sem, ds_sem, dr_sem, rs_sem, rr_sem, cs_sem, cr_sem,
):
    d = lax.axis_index("doc")
    c = lax.axis_index("cen")
    block, width = p_ref.shape
    cols = c_ref.shape[0]
    rows = nc * block
    feats = width // nd
    scale = math.log2(math.e) / math.sqrt(width)
    log_column = math.log2(rows * nd / (cols * nc))
    sends = []
    mate = c + 1 - 2 * lax.rem(c, 2)
    half = nc // 2
    beside = d + 1 - 2 * lax.rem(d, 2)
    docs = [d, beside, lax.rem(d + 2, nd), lax.rem(beside + 2, nd)]

    barrier = pltpu.get_barrier_semaphore()
    for k in range(1, nc):
        pl.semaphore_signal(barrier, inc=1, device_id=(d, lax.rem(c + k, nc)), device_id_type=MESH)
    for q in range(1, nd):
        pl.semaphore_signal(barrier, inc=1, device_id=(docs[q], c), device_id_type=MESH)
    load_p = pltpu.make_async_copy(p_ref, rows_v.at[0, c], load_sem.at[0])
    load_c = pltpu.make_async_copy(c_ref, cent_v, load_sem.at[1])
    load_p.start()
    load_c.start()
    pl.semaphore_wait(barrier, nc + nd - 2)

    def push(src, dst, send, recv, where):
        copy = pltpu.make_async_remote_copy(
            src_ref=src, dst_ref=dst, send_sem=send, recv_sem=recv, device_id=where, device_id_type=MESH
        )
        copy.start()
        sends.append(copy)

    def drain():
        for copy in sends:
            copy.wait_send()
        sends.clear()

    def arrive(ref, send, recv):
        pltpu.make_async_remote_copy(
            src_ref=ref, dst_ref=ref, send_sem=send, recv_sem=recv, device_id=(d, c), device_id_type=MESH
        ).wait_recv()

    z = c // 2
    near = c + 2 - 4 * lax.rem(z, 2)
    blocks = [c, near, lax.rem(c + half, nc), lax.rem(near + half, nc)]
    mates = [b + mate - c for b in blocks]
    tile = min(256, cols)

    def to_docs(src, k):
        for q in range(1, nd):
            push(src, rows_v.at[q, blocks[k]], ds_sem.at[q, k], dr_sem.at[q, blocks[k]], (docs[q], c))

    def take_block(k):
        got = rows_v.at[0, blocks[k]]
        arrive(got, gs_sem.at[half + k], gr_sem.at[blocks[k]])
        push(got, got, gs_sem.at[half + k], gr_sem.at[blocks[k]], (d, mate))
        if k < half - 1:
            to_docs(got, k)

    def take_mate(k):
        arrive(rows_v.at[0, mates[k]], gs_sem.at[0], gr_sem.at[mates[k]])

    def score_half(h):
        x = rows_v[0, pl.ds(h * half, half)].reshape(rows // 2, width)
        to = pl.ds(pl.multiple_of(h * (rows // 2), 32), rows // 2)
        for j in range(0, cols, tile):
            at = slice(j, j + tile)
            scores[0, to, at] = jnp.dot(x, cent_t[:, at], preferred_element_type=jnp.float32) * scale

    for k in range(1, half):
        push(p_ref, rows_v.at[0, c], gs_sem.at[k], gr_sem.at[c], (d, blocks[k]))
    push(p_ref, rows_v.at[0, c], gs_sem.at[0], gr_sem.at[c], (d, mate))
    to_docs(p_ref, 0)
    load_c.wait()
    cent_t[...] = cent_v[...].T
    load_p.wait()
    take_block(1)
    take_mate(0)
    take_mate(1)
    score_half(z // 2)
    take_block(2)
    take_block(3)
    take_mate(2)
    take_mate(3)
    score_half(1 - z // 2)

    def relay(k):
        for q in range(1, nd):
            got = rows_v.at[q, blocks[k]]
            arrive(got, ds_sem.at[0, k], dr_sem.at[q, blocks[k]])
            push(got, got, ds_sem.at[nd + q, k], dr_sem.at[q, blocks[k]], (d, mate))

    my_feats = pl.ds(pl.multiple_of(d * feats, feats), feats)

    def turn(q):
        pt_v[q] = rows_v[q, :, :, my_feats].reshape(rows, feats).T

    def take(q):
        for k in range(half):
            arrive(rows_v.at[q, mates[k]], ds_sem.at[0, k], dr_sem.at[q, mates[k]])
        x = rows_v[q].reshape(rows, width)
        for j in range(0, cols, tile):
            at = slice(j, j + tile)
            scores[q, :, at] = jnp.dot(x, cent_t[:, at], preferred_element_type=jnp.float32) * scale
        turn(q)

    def widen(x):
        return jnp.broadcast_to(x, (LANES, x.shape[1])).T

    step_rows = 32

    def row_stats(q, r, col_potential):
        for g in range(rows // LANES):
            parts = []
            for i in range(g * LANES, (g + 1) * LANES, step_rows):
                xs = []
                for j in range(0, cols, LANES):
                    x = scores[q, i : i + step_rows, j : j + LANES]
                    if col_potential is not None:
                        x = x + col_potential[:, j : j + LANES]
                    xs.append(x)
                m = functools.reduce(jnp.maximum, xs)
                s = functools.reduce(jnp.add, [jnp.exp2(x - m) for x in xs])
                parts.append(m + jnp.log2(s))
            t = jnp.concatenate(parts, axis=0).T
            m = jnp.max(t, axis=0, keepdims=True)
            s = jnp.sum(jnp.exp2(t - m), axis=0, keepdims=True)
            row_slots[r, q, c, :, g * LANES : (g + 1) * LANES] = m + jnp.log2(s)
        mine = row_slots.at[r, q, c]
        for k in range(1, nc):
            push(mine, mine, rs_sem.at[r, q, k], rr_sem.at[r, q, c], (d, lax.rem(c + k, nc)))

    def join(parts):
        peak = functools.reduce(jnp.maximum, parts)
        return peak + jnp.log2(functools.reduce(jnp.add, [jnp.exp2(x - peak) for x in parts]))

    def row_potential(q, r):
        for k in range(1, nc):
            src = lax.rem(c + nc - k, nc)
            arrive(row_slots.at[r, q, src], rs_sem.at[r, q, 0], rr_sem.at[r, q, src])
        return -join([row_slots[r, q, k] for k in range(nc)])

    def col_part(q, r):
        rexp[...] = widen(row_potential(q, r))
        for j in range(0, cols, LANES):
            ms, ss = [], []
            for i in range(0, rows, LANES):
                x = scores[q, i : i + LANES, j : j + LANES] + rexp[i : i + LANES, :]
                x = x.reshape(LANES // 8, 8, LANES)
                m = jnp.max(x, axis=0)
                ms.append(m)
                ss.append(jnp.sum(jnp.exp2(x - m[None]), axis=0))
            m = functools.reduce(jnp.maximum, ms)
            cm[q, :, j : j + LANES] = m
            cs[q, :, j : j + LANES] = functools.reduce(jnp.add, [s * jnp.exp2(a - m) for a, s in zip(ms, ss)])

    def col_merge(n):
        peak = jnp.max(jnp.max(cm[0:n], axis=0), axis=0, keepdims=True)
        total = functools.reduce(jnp.add, [cs[q] * jnp.exp2(cm[q] - peak) for q in range(n)])
        return peak + jnp.log2(jnp.sum(total, axis=0, keepdims=True))

    def split_round(r, col_potential, before, after):
        row_stats(0, r, col_potential)
        before()
        col_part(0, r)
        col_slots[r, 0] = col_merge(1)
        for q in range(1, nd):
            push(col_slots.at[r, 0], col_slots.at[r, q], cs_sem.at[r, q], cr_sem.at[r, q], (docs[q], c))
        after()
        for q in range(1, nd):
            arrive(col_slots.at[r, q], cs_sem.at[r, 0], cr_sem.at[r, q])
        return log_column - join([col_slots[r, q] for q in range(nd)])

    def whole_round(r, col_potential):
        for q in range(nd):
            row_stats(q, r, col_potential)
        drain()
        for q in range(nd):
            col_part(q, r)
        return log_column - col_merge(nd)

    col_potential = None
    plan = [[(0, 0), (0, 1)], [(3, 3), (2, 0)], [(0, 2), (0, 3)], [(1, 1), (1, 2), (1, 3)]]
    jobs = {0: relay, 1: take, 2: turn, 3: lambda k: to_docs(rows_v.at[0, blocks[k]], k)}
    work = [lambda todo=todo: [jobs[a](b) for a, b in todo] for todo in plan]
    for r in range(SPLIT_ROUNDS):
        col_potential = split_round(r, col_potential, *work[2 * r : 2 * r + 2])
    for r in range(SPLIT_ROUNDS, ITERS):
        col_potential = whole_round(r, col_potential)

    for q in range(nd):
        row_stats(q, ITERS, col_potential)
    for q in range(nd):
        rexp[...] = widen(row_slots[ITERS, q, c])
        for j in range(0, cols, LANES):
            at = slice(j, j + LANES)
            e = jnp.exp2(scores[q, :, at] + col_potential[:, at] - rexp[...])
            e_v[q, :, at] = e.astype(jnp.bfloat16)
            if not q:
                own_v[:, at] = e
    drain()
    pad = lhs.shape[0] - feats
    lane = lax.broadcasted_iota(jnp.int32, (pad, rows), 0)
    for q in range(nd):
        f = jnp.exp2(row_slots[ITERS, q, c] + row_potential(q, ITERS))
        lhs[0:feats, :] = (pt_v[q].astype(jnp.float32) * f).astype(jnp.bfloat16)
        high = f.astype(jnp.bfloat16).astype(jnp.float32)
        lhs[feats:, :] = jnp.where(lane == 0, high, jnp.where(lane == 1, f - high, 0.0)).astype(jnp.bfloat16)
        for j in range(0, cols, tile):
            at = slice(j, j + tile)
            part = jnp.dot(lhs[...], e_v[q, :, at], preferred_element_type=jnp.float32)
            acc_out[:, at] = acc_out[:, at] + part if q else part
        if not q:
            rexp[...] = widen(f * (cols * nc))
            for j in range(0, cols, LANES):
                at = slice(j, j + LANES)
                assign_out[:, at] = (own_v[:, at] * rexp[...]).astype(jnp.bfloat16)


def finish_kernel(total_rows, total_cols, assign_ref, acc, assign_out, mass_out, newc_out, mass_v, newc_v, out_sem):
    cols = assign_ref.shape[1]
    feats = newc_out.shape[1]
    copies = [pltpu.make_async_copy(assign_ref, assign_out, out_sem.at[0])]
    copies[0].start()
    for j in range(0, cols, LANES):
        at = slice(j, j + LANES)
        mass = acc[feats : feats + 1, at] + acc[feats + 1 : feats + 2, at]
        mass_v[j // LANES : j // LANES + 1, :] = mass * total_cols / total_rows
        newc_v[at, :] = (acc[0:feats, at] / mass).T
        if (j + LANES) % (2 * LANES) == 0:
            part = pl.ds(j - LANES, 2 * LANES)
            copies.append(
                pltpu.make_async_copy(newc_v.at[part], newc_out.at[part], out_sem.at[2 + j // (2 * LANES)])
            )
            copies[-1].start()
    copies.append(pltpu.make_async_copy(mass_v, mass_out, out_sem.at[1]))
    copies[-1].start()
    for copy in copies:
        copy.wait()


def wide_shards(nd, nc, passages, centroids):
    block, width = passages.shape
    cols = centroids.shape[0]
    rows = nc * block
    feats = width // nd
    dma = pltpu.SemaphoreType.DMA
    f32, bf16 = jnp.float32, jnp.bfloat16
    vmem = pl.BlockSpec(memory_space=pltpu.VMEM)
    any_spec = pl.BlockSpec(memory_space=pl.ANY)
    hbm = pltpu.MemorySpace.HBM
    passages, centroids = (pltpu.with_memory_space_constraint(x, hbm) for x in (passages, centroids))
    pad = 16
    assign, acc = pl.pallas_call(
        functools.partial(wide_kernel, nd, nc),
        out_shape=(
            jax.ShapeDtypeStruct((rows, cols), bf16),
            jax.ShapeDtypeStruct((feats + pad, cols), f32),
        ),
        in_specs=[pl.BlockSpec(memory_space=hbm)] * 2,
        out_specs=(vmem,) * 2,
        scratch_shapes=[
            pltpu.VMEM((nd, nc, block, width), bf16),
            pltpu.VMEM((cols, width), bf16),
            pltpu.VMEM((width, cols), bf16),
            pltpu.VMEM((nd, rows, cols), bf16),
            pltpu.VMEM((rows, cols), f32),
            pltpu.VMEM((nd, feats, rows), bf16),
            pltpu.VMEM((feats + pad, rows), bf16),
            pltpu.VMEM((nd, rows, cols), f32),
            pltpu.VMEM((rows, LANES), f32),
            pltpu.VMEM((ITERS + 1, nd, nc, 1, rows), f32),
            pltpu.VMEM((ITERS, nd, 1, cols), f32),
            pltpu.VMEM((nd, 8, cols), f32),
            pltpu.VMEM((nd, 8, cols), f32),
            dma((2,)),
            dma((nc,)),
            dma((nc,)),
            dma((2 * nd, nc // 2)),
            dma((nd, nc)),
            dma((ITERS + 1, nd, nc)),
            dma((ITERS + 1, nd, nc)),
            dma((ITERS, nd)),
            dma((ITERS, nd)),
        ],
        compiler_params=pltpu.CompilerParams(
            collective_id=0, has_side_effects=True, vmem_limit_bytes=44 * 1024 * 1024
        ),
    )(passages, centroids)
    assign, masses, newc = pl.pallas_call(
        functools.partial(finish_kernel, rows * nd, cols * nc),
        out_shape=(
            jax.ShapeDtypeStruct((rows, cols), bf16),
            jax.ShapeDtypeStruct((cols // LANES, LANES), f32),
            jax.ShapeDtypeStruct((cols, feats), f32),
        ),
        in_specs=[vmem] * 2,
        out_specs=(any_spec,) * 3,
        scratch_shapes=[
            pltpu.VMEM((cols // LANES, LANES), f32),
            pltpu.VMEM((cols, feats), f32),
            dma((2 + cols // (2 * LANES),)),
        ],
        compiler_params=pltpu.CompilerParams(vmem_limit_bytes=32 * 1024 * 1024),
    )(assign, acc)
    return assign, masses.reshape(cols), newc


def shards(nd, nc, passages, centroids):
    block, width = passages.shape
    cols = centroids.shape[0]
    rows = nc * block
    feats = width // nd
    if nd == 4 and nc == 8 and nd * rows * cols <= 2**21 and rows % LANES == 0 and cols % 256 == 0:
        return wide_shards(nd, nc, passages, centroids)
    any_spec = pl.BlockSpec(memory_space=pl.ANY)
    dma = pltpu.SemaphoreType.DMA
    f32, bf16 = jnp.float32, jnp.bfloat16
    assign, masses, newc = pl.pallas_call(
        functools.partial(kernel, nd, nc),
        out_shape=(
            jax.ShapeDtypeStruct((rows, cols), bf16),
            jax.ShapeDtypeStruct((1, cols), f32),
            jax.ShapeDtypeStruct((cols, feats), f32),
        ),
        in_specs=[pl.BlockSpec(memory_space=pltpu.MemorySpace.HBM)] * 2,
        out_specs=(any_spec, pl.BlockSpec(memory_space=pltpu.VMEM), any_spec),
        scratch_shapes=[
            pltpu.VMEM((nc, block, width), bf16),
            pltpu.VMEM((cols, width), bf16),
            pltpu.VMEM((rows, cols), f32),
            pltpu.VMEM((rows, LANES), f32),
            pltpu.VMEM((rows, LANES), f32),
            pltpu.VMEM((ITERS + 1, nc, 2, rows), f32),
            pltpu.VMEM((ITERS, nd, 2, cols), f32),
            pltpu.VMEM((nd, 1, cols), f32),
            pltpu.VMEM((rows, cols), bf16),
            pltpu.VMEM((nd, cols, feats), bf16),
            pltpu.VMEM((nd, cols, feats), bf16),
            pltpu.VMEM((cols, feats), f32),
            dma((2,)),
            dma((nc,)),
            dma((nc,)),
            dma((ITERS + 1, nc)),
            dma((ITERS + 1, nc)),
            dma((ITERS, nd)),
            dma((ITERS, nd)),
            dma((nd,)),
            dma((nd,)),
            dma((nd,)),
            dma((nd,)),
            dma((2,)),
        ],
        compiler_params=pltpu.CompilerParams(
            collective_id=0, has_side_effects=True, vmem_limit_bytes=52 * 1024 * 1024
        ),
    )(passages, centroids)
    return assign, masses.reshape(cols), newc


def solution(mesh):
    nd, nc = mesh.shape["doc"], mesh.shape["cen"]
    in_specs = (P(("doc", "cen"), None), P("cen", None))
    out_specs = (P("doc", "cen"), P("cen"), P("cen", "doc"))
    return jax.shard_map(
        functools.partial(shards, nd, nc), mesh=mesh, in_specs=in_specs, out_specs=out_specs, check_vma=False
    )
```

```python
import functools
import math

import jax
import jax.numpy as jnp
from jax import lax
from jax.experimental import pallas as pl
from jax.experimental.pallas import tpu as pltpu
from jax.sharding import PartitionSpec as P

ITERS = 3
MESH = pl.DeviceIdType.MESH
LANES = 128


def kernel(
    nd, nc, p_ref, c_ref, assign_out, mass_out, newc_out,
    rows_v, cent_v, scores, rp_v, tbuf, row_slots, col_slots, mass_slots, assign_v, part_send, part_recv, newc_v,
    load_sem, gs_sem, gr_sem, rs_sem, rr_sem, cs_sem, cr_sem, ms_sem, mr_sem, ps_sem, pr_sem, out_sem,
):
    d = lax.axis_index("doc")
    c = lax.axis_index("cen")
    block, width = p_ref.shape
    cols = c_ref.shape[0]
    rows = nc * block
    feats = width // nd
    total_cols = cols * nc
    total_rows = rows * nd
    scale = 1.0 / math.sqrt(width)
    log_column = math.log(total_rows / total_cols)
    sends = []

    load_p = pltpu.make_async_copy(p_ref, rows_v.at[c], load_sem.at[0])
    load_c = pltpu.make_async_copy(c_ref, cent_v, load_sem.at[1])
    load_p.start()
    load_c.start()

    barrier = pltpu.get_barrier_semaphore()
    for k in range(1, nc):
        pl.semaphore_signal(barrier, inc=1, device_id=(d, lax.rem(c + k, nc)), device_id_type=MESH)
    for k in range(1, nd):
        pl.semaphore_signal(barrier, inc=1, device_id=(lax.rem(d + k, nd), c), device_id_type=MESH)
    pl.semaphore_wait(barrier, nc + nd - 2)
    load_p.wait()

    def push(src, dst, send, recv, where):
        copy = pltpu.make_async_remote_copy(
            src_ref=src, dst_ref=dst, send_sem=send, recv_sem=recv, device_id=where, device_id_type=MESH
        )
        copy.start()
        sends.append(copy)

    def arrive(ref, send, recv):
        pltpu.make_async_remote_copy(
            src_ref=ref, dst_ref=ref, send_sem=send, recv_sem=recv, device_id=(d, c), device_id_type=MESH
        ).wait_recv()

    mate = c + 1 - 2 * lax.rem(c, 2)
    half = nc // 2
    for k in range(1, half):
        push(rows_v.at[c], rows_v.at[c], gs_sem.at[k], gr_sem.at[c], (d, lax.rem(c + 2 * k, nc)))
    push(rows_v.at[c], rows_v.at[c], gs_sem.at[0], gr_sem.at[c], (d, mate))
    order = [k for pair in zip(range(1, half), reversed(range(1, half))) for k in pair][: half - 1]
    for k in order:
        src = lax.rem(c + nc - 2 * k, nc)
        arrive(rows_v.at[src], gs_sem.at[half + k], gr_sem.at[src])
        push(rows_v.at[src], rows_v.at[src], gs_sem.at[half + k], gr_sem.at[src], (d, mate))
    arrive(rows_v.at[mate], gs_sem.at[0], gr_sem.at[mate])
    for k in range(1, half):
        src = lax.rem(mate + nc - 2 * k, nc)
        arrive(rows_v.at[src], gs_sem.at[0], gr_sem.at[src])
    load_c.wait()

    group_rows = rows_v[...].reshape(rows, width)
    tile = min(256, cols)
    for j in range(cols // tile):
        at = slice(j * tile, (j + 1) * tile)
        scores[:, at] = (
            lax.dot_general(
                group_rows, cent_v[at, :], (((1,), (1,)), ((), ())), preferred_element_type=jnp.float32
            )
            * scale
        )

    step_rows = 64
    lane = lax.broadcasted_iota(jnp.int32, (step_rows, LANES), 1)

    def combine(slots, r, n):
        peak = slots[r, 0, 0:1, :]
        for k in range(1, n):
            peak = jnp.maximum(peak, slots[r, k, 0:1, :])
        total = jnp.zeros_like(peak)
        for k in range(n):
            total = total + slots[r, k, 1:2, :] * jnp.exp(slots[r, k, 0:1, :] - peak)
        return peak + jnp.log(total)

    def row_round(r, col_potential):
        @pl.loop(0, rows // step_rows)
        def _(i):
            at = pl.ds(pl.multiple_of(i * step_rows, step_rows), step_rows)
            x = scores[at, :]
            if col_potential is not None:
                x = x + col_potential
            m = jnp.max(x, axis=1, keepdims=True)
            s = jnp.sum(jnp.exp(x - m), axis=1, keepdims=True)
            tbuf[at, :] = jnp.where(lane == 0, m, s)

        row_slots[r, c, :, :] = tbuf[...].T[0:2, :]
        for k in range(1, nc):
            push(row_slots.at[r, c], row_slots.at[r, c], rs_sem.at[r, k], rr_sem.at[r, c], (d, lax.rem(c + k, nc)))
        for k in range(1, nc):
            src = lax.rem(c + nc - k, nc)
            arrive(row_slots.at[r, src], rs_sem.at[r, k], rr_sem.at[r, src])
        row_potential = -combine(row_slots, r, nc)
        rp_v[...] = jnp.broadcast_to(row_potential, (LANES, rows)).T

    def col_round(r):
        for j in range(cols // LANES):
            at = slice(j * LANES, (j + 1) * LANES)
            x = scores[:, at] + rp_v[...]
            m = jnp.max(x, axis=0, keepdims=True)
            s = jnp.sum(jnp.exp(x - m), axis=0, keepdims=True)
            col_slots[r, d, 0:1, at] = m
            col_slots[r, d, 1:2, at] = s
        for k in range(1, nd):
            push(col_slots.at[r, d], col_slots.at[r, d], cs_sem.at[r, k], cr_sem.at[r, d], (lax.rem(d + k, nd), c))
        for k in range(1, nd):
            src = lax.rem(d + nd - k, nd)
            arrive(col_slots.at[r, src], cs_sem.at[r, k], cr_sem.at[r, src])
        return log_column - combine(col_slots, r, nd)

    col_potential = None
    for r in range(ITERS):
        row_round(r, col_potential)
        col_potential = col_round(r)
    row_round(ITERS, col_potential)

    for j in range(cols // LANES):
        at = slice(j * LANES, (j + 1) * LANES)
        w = jnp.exp(scores[:, at] + rp_v[...] + col_potential[:, at])
        mass_slots[d, :, at] = jnp.sum(w, axis=0, keepdims=True)
        assign_v[:, at] = (w * total_cols).astype(jnp.bfloat16)
    assign_copy = pltpu.make_async_copy(assign_v, assign_out, out_sem.at[0])
    assign_copy.start()
    for k in range(1, nd):
        push(mass_slots.at[d], mass_slots.at[d], ms_sem.at[k], mr_sem.at[d], (lax.rem(d + k, nd), c))

    def partial(q):
        r3 = rows_v[:, :, pl.ds(pl.multiple_of(q * feats, feats), feats)].reshape(rows, feats)
        return lax.dot_general(
            assign_v[...], r3, (((0,), (0,)), ((), ())), preferred_element_type=jnp.float32
        ).astype(jnp.bfloat16)

    for k in reversed(range(1, nd)):
        q = lax.rem(d + k, nd)
        part_send[k, :, :] = partial(q)
        push(part_send.at[k], part_recv.at[d], ps_sem.at[k], pr_sem.at[d], (q, c))
    part_recv[d, :, :] = partial(d)

    for k in range(1, nd):
        src = lax.rem(d + nd - k, nd)
        arrive(mass_slots.at[src], ms_sem.at[k], mr_sem.at[src])
    raw_mass = mass_slots[0]
    for k in range(1, nd):
        raw_mass = raw_mass + mass_slots[k]
    mass_out[...] = raw_mass * total_cols / total_rows
    mass_col = jnp.broadcast_to(raw_mass, (LANES, cols)).T

    for k in range(1, nd):
        src = lax.rem(d + nd - k, nd)
        arrive(part_recv.at[src], ps_sem.at[k], pr_sem.at[src])
    for j in range(feats // LANES):
        at = slice(j * LANES, (j + 1) * LANES)
        sums = part_recv[0, :, at].astype(jnp.float32)
        for k in range(1, nd):
            sums = sums + part_recv[k, :, at].astype(jnp.float32)
        newc_v[:, at] = sums / total_cols / mass_col
    newc_copy = pltpu.make_async_copy(newc_v, newc_out, out_sem.at[1])
    newc_copy.start()
    for copy in sends:
        copy.wait_send()
    assign_copy.wait()
    newc_copy.wait()


SPLIT_ROUNDS = 2


def wide_kernel(
    nd, nc, p_ref, c_ref, assign_out, acc_out,
    rows_v, cent_v, cent_t, e_v, own_v, pt_v, lhs, scores, rexp, row_slots, col_slots, cm, cs,
    load_sem, gs_sem, gr_sem, ds_sem, dr_sem, rs_sem, rr_sem, cs_sem, cr_sem,
):
    d = lax.axis_index("doc")
    c = lax.axis_index("cen")
    block, width = p_ref.shape
    cols = c_ref.shape[0]
    rows = nc * block
    feats = width // nd
    scale = math.log2(math.e) / math.sqrt(width)
    log_column = math.log2(rows * nd / (cols * nc))
    sends = []
    mate = c + 1 - 2 * lax.rem(c, 2)
    half = nc // 2
    beside = d + 1 - 2 * lax.rem(d, 2)
    docs = [d, beside, lax.rem(d + 2, nd), lax.rem(beside + 2, nd)]

    barrier = pltpu.get_barrier_semaphore()
    for k in range(1, nc):
        pl.semaphore_signal(barrier, inc=1, device_id=(d, lax.rem(c + k, nc)), device_id_type=MESH)
    for q in range(1, nd):
        pl.semaphore_signal(barrier, inc=1, device_id=(docs[q], c), device_id_type=MESH)
    load_p = pltpu.make_async_copy(p_ref, rows_v.at[0, c], load_sem.at[0])
    load_c = pltpu.make_async_copy(c_ref, cent_v, load_sem.at[1])
    load_p.start()
    load_c.start()
    pl.semaphore_wait(barrier, nc + nd - 2)

    def push(src, dst, send, recv, where):
        copy = pltpu.make_async_remote_copy(
            src_ref=src, dst_ref=dst, send_sem=send, recv_sem=recv, device_id=where, device_id_type=MESH
        )
        copy.start()
        sends.append(copy)

    def drain():
        for copy in sends:
            copy.wait_send()
        sends.clear()

    def arrive(ref, send, recv):
        pltpu.make_async_remote_copy(
            src_ref=ref, dst_ref=ref, send_sem=send, recv_sem=recv, device_id=(d, c), device_id_type=MESH
        ).wait_recv()

    z = c // 2
    near = c + 2 - 4 * lax.rem(z, 2)
    blocks = [c, near, lax.rem(c + half, nc), lax.rem(near + half, nc)]
    mates = [b + mate - c for b in blocks]
    tile = min(256, cols)

    def to_docs(src, k):
        for q in range(1, nd):
            push(src, rows_v.at[q, blocks[k]], ds_sem.at[q, k], dr_sem.at[q, blocks[k]], (docs[q], c))

    def take_block(k):
        got = rows_v.at[0, blocks[k]]
        arrive(got, gs_sem.at[half + k], gr_sem.at[blocks[k]])
        push(got, got, gs_sem.at[half + k], gr_sem.at[blocks[k]], (d, mate))
        if k < half - 1:
            to_docs(got, k)

    def take_mate(k):
        arrive(rows_v.at[0, mates[k]], gs_sem.at[0], gr_sem.at[mates[k]])

    def score_half(h):
        x = rows_v[0, pl.ds(h * half, half)].reshape(rows // 2, width)
        to = pl.ds(pl.multiple_of(h * (rows // 2), 32), rows // 2)
        for j in range(0, cols, tile):
            at = slice(j, j + tile)
            scores[0, to, at] = jnp.dot(x, cent_t[:, at], preferred_element_type=jnp.float32) * scale

    for k in range(1, half):
        push(p_ref, rows_v.at[0, c], gs_sem.at[k], gr_sem.at[c], (d, blocks[k]))
    push(p_ref, rows_v.at[0, c], gs_sem.at[0], gr_sem.at[c], (d, mate))
    to_docs(p_ref, 0)
    load_c.wait()
    cent_t[...] = cent_v[...].T
    load_p.wait()
    take_block(1)
    take_mate(0)
    take_mate(1)
    score_half(z // 2)
    take_block(2)
    take_block(3)
    take_mate(2)
    take_mate(3)
    score_half(1 - z // 2)

    def relay(k):
        for q in range(1, nd):
            got = rows_v.at[q, blocks[k]]
            arrive(got, ds_sem.at[0, k], dr_sem.at[q, blocks[k]])
            push(got, got, ds_sem.at[nd + q, k], dr_sem.at[q, blocks[k]], (d, mate))

    my_feats = pl.ds(pl.multiple_of(d * feats, feats), feats)

    def turn(q):
        pt_v[q] = rows_v[q, :, :, my_feats].reshape(rows, feats).T

    def take(q):
        for k in range(half):
            arrive(rows_v.at[q, mates[k]], ds_sem.at[0, k], dr_sem.at[q, mates[k]])
        x = rows_v[q].reshape(rows, width)
        for j in range(0, cols, tile):
            at = slice(j, j + tile)
            scores[q, :, at] = jnp.dot(x, cent_t[:, at], preferred_element_type=jnp.float32) * scale
        turn(q)

    def widen(x):
        return jnp.broadcast_to(x, (LANES, x.shape[1])).T

    step_rows = 32

    def row_stats(q, r, col_potential):
        for g in range(rows // LANES):
            parts = []
            for i in range(g * LANES, (g + 1) * LANES, step_rows):
                xs = []
                for j in range(0, cols, LANES):
                    x = scores[q, i : i + step_rows, j : j + LANES]
                    if col_potential is not None:
                        x = x + col_potential[:, j : j + LANES]
                    xs.append(x)
                m = functools.reduce(jnp.maximum, xs)
                s = functools.reduce(jnp.add, [jnp.exp2(x - m) for x in xs])
                parts.append(m + jnp.log2(s))
            t = jnp.concatenate(parts, axis=0).T
            m = jnp.max(t, axis=0, keepdims=True)
            s = jnp.sum(jnp.exp2(t - m), axis=0, keepdims=True)
            row_slots[r, q, c, :, g * LANES : (g + 1) * LANES] = m + jnp.log2(s)
        mine = row_slots.at[r, q, c]
        for k in range(1, nc):
            push(mine, mine, rs_sem.at[r, q, k], rr_sem.at[r, q, c], (d, lax.rem(c + k, nc)))

    def join(parts):
        peak = functools.reduce(jnp.maximum, parts)
        return peak + jnp.log2(functools.reduce(jnp.add, [jnp.exp2(x - peak) for x in parts]))

    def row_potential(q, r):
        for k in range(1, nc):
            src = lax.rem(c + nc - k, nc)
            arrive(row_slots.at[r, q, src], rs_sem.at[r, q, 0], rr_sem.at[r, q, src])
        return -join([row_slots[r, q, k] for k in range(nc)])

    def col_part(q, r):
        rexp[...] = widen(row_potential(q, r))
        for j in range(0, cols, LANES):
            ms, ss = [], []
            for i in range(0, rows, LANES):
                x = scores[q, i : i + LANES, j : j + LANES] + rexp[i : i + LANES, :]
                x = x.reshape(LANES // 8, 8, LANES)
                m = jnp.max(x, axis=0)
                ms.append(m)
                ss.append(jnp.sum(jnp.exp2(x - m[None]), axis=0))
            m = functools.reduce(jnp.maximum, ms)
            cm[q, :, j : j + LANES] = m
            cs[q, :, j : j + LANES] = functools.reduce(jnp.add, [s * jnp.exp2(a - m) for a, s in zip(ms, ss)])

    def col_merge(n):
        peak = jnp.max(jnp.max(cm[0:n], axis=0), axis=0, keepdims=True)
        total = functools.reduce(jnp.add, [cs[q] * jnp.exp2(cm[q] - peak) for q in range(n)])
        return peak + jnp.log2(jnp.sum(total, axis=0, keepdims=True))

    def split_round(r, col_potential, before, after):
        row_stats(0, r, col_potential)
        before()
        col_part(0, r)
        col_slots[r, 0] = col_merge(1)
        for q in range(1, nd):
            push(col_slots.at[r, 0], col_slots.at[r, q], cs_sem.at[r, q], cr_sem.at[r, q], (docs[q], c))
        after()
        for q in range(1, nd):
            arrive(col_slots.at[r, q], cs_sem.at[r, 0], cr_sem.at[r, q])
        return log_column - join([col_slots[r, q] for q in range(nd)])

    def whole_round(r, col_potential):
        for q in range(nd):
            row_stats(q, r, col_potential)
        drain()
        for q in range(nd):
            col_part(q, r)
        return log_column - col_merge(nd)

    col_potential = None
    plan = [[(0, 0), (0, 1)], [(3, 3), (2, 0)], [(0, 2), (0, 3)], [(1, 1), (1, 2), (1, 3)]]
    jobs = {0: relay, 1: take, 2: turn, 3: lambda k: to_docs(rows_v.at[0, blocks[k]], k)}
    work = [lambda todo=todo: [jobs[a](b) for a, b in todo] for todo in plan]
    for r in range(SPLIT_ROUNDS):
        col_potential = split_round(r, col_potential, *work[2 * r : 2 * r + 2])
    for r in range(SPLIT_ROUNDS, ITERS):
        col_potential = whole_round(r, col_potential)

    for q in range(nd):
        row_stats(q, ITERS, col_potential)
    for q in range(nd):
        rexp[...] = widen(row_slots[ITERS, q, c])
        for j in range(0, cols, LANES):
            at = slice(j, j + LANES)
            e = jnp.exp2(scores[q, :, at] + col_potential[:, at] - rexp[...])
            e_v[q, :, at] = e.astype(jnp.bfloat16)
            if not q:
                own_v[:, at] = e
    drain()
    pad = lhs.shape[0] - feats
    lane = lax.broadcasted_iota(jnp.int32, (pad, rows), 0)
    for q in range(nd):
        f = jnp.exp2(row_slots[ITERS, q, c] + row_potential(q, ITERS))
        if not q:
            rexp[...] = widen(f * (cols * nc))
            for j in range(0, cols, LANES):
                at = slice(j, j + LANES)
                assign_out[:, at] = (own_v[:, at] * rexp[...]).astype(jnp.bfloat16)
        lhs[0:feats, :] = (pt_v[q].astype(jnp.float32) * f).astype(jnp.bfloat16)
        high = f.astype(jnp.bfloat16).astype(jnp.float32)
        lhs[feats:, :] = jnp.where(lane == 0, high, jnp.where(lane == 1, f - high, 0.0)).astype(jnp.bfloat16)
        for j in range(0, cols, tile):
            at = slice(j, j + tile)
            part = jnp.dot(lhs[...], e_v[q, :, at], preferred_element_type=jnp.float32)
            acc_out[:, at] = acc_out[:, at] + part if q else part


def finish_kernel(total_rows, total_cols, assign_ref, acc, assign_out, mass_out, newc_out, mass_v, newc_v, out_sem):
    cols = assign_ref.shape[1]
    feats = newc_out.shape[1]
    copies = [pltpu.make_async_copy(assign_ref, assign_out, out_sem.at[0])]
    copies[0].start()
    for j in range(0, cols, LANES):
        at = slice(j, j + LANES)
        mass = acc[feats : feats + 1, at] + acc[feats + 1 : feats + 2, at]
        mass_v[j // LANES : j // LANES + 1, :] = mass * total_cols / total_rows
        newc_v[at, :] = (acc[0:feats, at] / mass).T
        if (j + LANES) % (2 * LANES) == 0:
            part = pl.ds(j - LANES, 2 * LANES)
            copies.append(
                pltpu.make_async_copy(newc_v.at[part], newc_out.at[part], out_sem.at[2 + j // (2 * LANES)])
            )
            copies[-1].start()
    copies.append(pltpu.make_async_copy(mass_v, mass_out, out_sem.at[1]))
    copies[-1].start()
    for copy in copies:
        copy.wait()


def wide_shards(nd, nc, passages, centroids):
    block, width = passages.shape
    cols = centroids.shape[0]
    rows = nc * block
    feats = width // nd
    dma = pltpu.SemaphoreType.DMA
    f32, bf16 = jnp.float32, jnp.bfloat16
    vmem = pl.BlockSpec(memory_space=pltpu.VMEM)
    any_spec = pl.BlockSpec(memory_space=pl.ANY)
    hbm = pltpu.MemorySpace.HBM
    passages, centroids = (pltpu.with_memory_space_constraint(x, hbm) for x in (passages, centroids))
    pad = 16
    assign, acc = pl.pallas_call(
        functools.partial(wide_kernel, nd, nc),
        out_shape=(
            jax.ShapeDtypeStruct((rows, cols), bf16),
            jax.ShapeDtypeStruct((feats + pad, cols), f32),
        ),
        in_specs=[pl.BlockSpec(memory_space=hbm)] * 2,
        out_specs=(vmem,) * 2,
        scratch_shapes=[
            pltpu.VMEM((nd, nc, block, width), bf16),
            pltpu.VMEM((cols, width), bf16),
            pltpu.VMEM((width, cols), bf16),
            pltpu.VMEM((nd, rows, cols), bf16),
            pltpu.VMEM((rows, cols), f32),
            pltpu.VMEM((nd, feats, rows), bf16),
            pltpu.VMEM((feats + pad, rows), bf16),
            pltpu.VMEM((nd, rows, cols), f32),
            pltpu.VMEM((rows, LANES), f32),
            pltpu.VMEM((ITERS + 1, nd, nc, 1, rows), f32),
            pltpu.VMEM((ITERS, nd, 1, cols), f32),
            pltpu.VMEM((nd, 8, cols), f32),
            pltpu.VMEM((nd, 8, cols), f32),
            dma((2,)),
            dma((nc,)),
            dma((nc,)),
            dma((2 * nd, nc // 2)),
            dma((nd, nc)),
            dma((ITERS + 1, nd, nc)),
            dma((ITERS + 1, nd, nc)),
            dma((ITERS, nd)),
            dma((ITERS, nd)),
        ],
        compiler_params=pltpu.CompilerParams(
            collective_id=0, has_side_effects=True, vmem_limit_bytes=44 * 1024 * 1024
        ),
    )(passages, centroids)
    assign, masses, newc = pl.pallas_call(
        functools.partial(finish_kernel, rows * nd, cols * nc),
        out_shape=(
            jax.ShapeDtypeStruct((rows, cols), bf16),
            jax.ShapeDtypeStruct((cols // LANES, LANES), f32),
            jax.ShapeDtypeStruct((cols, feats), f32),
        ),
        in_specs=[vmem] * 2,
        out_specs=(any_spec,) * 3,
        scratch_shapes=[
            pltpu.VMEM((cols // LANES, LANES), f32),
            pltpu.VMEM((cols, feats), f32),
            dma((2 + cols // (2 * LANES),)),
        ],
        compiler_params=pltpu.CompilerParams(vmem_limit_bytes=32 * 1024 * 1024),
    )(assign, acc)
    return assign, masses.reshape(cols), newc


def shards(nd, nc, passages, centroids):
    block, width = passages.shape
    cols = centroids.shape[0]
    rows = nc * block
    feats = width // nd
    if nd == 4 and nc == 8 and nd * rows * cols <= 2**21 and rows % LANES == 0 and cols % 256 == 0:
        return wide_shards(nd, nc, passages, centroids)
    any_spec = pl.BlockSpec(memory_space=pl.ANY)
    dma = pltpu.SemaphoreType.DMA
    f32, bf16 = jnp.float32, jnp.bfloat16
    assign, masses, newc = pl.pallas_call(
        functools.partial(kernel, nd, nc),
        out_shape=(
            jax.ShapeDtypeStruct((rows, cols), bf16),
            jax.ShapeDtypeStruct((1, cols), f32),
            jax.ShapeDtypeStruct((cols, feats), f32),
        ),
        in_specs=[pl.BlockSpec(memory_space=pltpu.MemorySpace.HBM)] * 2,
        out_specs=(any_spec, pl.BlockSpec(memory_space=pltpu.VMEM), any_spec),
        scratch_shapes=[
            pltpu.VMEM((nc, block, width), bf16),
            pltpu.VMEM((cols, width), bf16),
            pltpu.VMEM((rows, cols), f32),
            pltpu.VMEM((rows, LANES), f32),
            pltpu.VMEM((rows, LANES), f32),
            pltpu.VMEM((ITERS + 1, nc, 2, rows), f32),
            pltpu.VMEM((ITERS, nd, 2, cols), f32),
            pltpu.VMEM((nd, 1, cols), f32),
            pltpu.VMEM((rows, cols), bf16),
            pltpu.VMEM((nd, cols, feats), bf16),
            pltpu.VMEM((nd, cols, feats), bf16),
            pltpu.VMEM((cols, feats), f32),
            dma((2,)),
            dma((nc,)),
            dma((nc,)),
            dma((ITERS + 1, nc)),
            dma((ITERS + 1, nc)),
            dma((ITERS, nd)),
            dma((ITERS, nd)),
            dma((nd,)),
            dma((nd,)),
            dma((nd,)),
            dma((nd,)),
            dma((2,)),
        ],
        compiler_params=pltpu.CompilerParams(
            collective_id=0, has_side_effects=True, vmem_limit_bytes=52 * 1024 * 1024
        ),
    )(passages, centroids)
    return assign, masses.reshape(cols), newc


def solution(mesh):
    nd, nc = mesh.shape["doc"], mesh.shape["cen"]
    in_specs = (P(("doc", "cen"), None), P("cen", None))
    out_specs = (P("doc", "cen"), P("cen"), P("cen", "doc"))
    return jax.shard_map(
        functools.partial(shards, nd, nc), mesh=mesh, in_specs=in_specs, out_specs=out_specs, check_vma=False
    )
```
